32 devices in a mesh: groups: 2 (over y), gx: 4 (over z), gy: 2 (over x), gz: 2 (over core).
Axes of the slice: x: 2, y: 2, z: 4, core: 2. Of those that a mesh axis runs over, the one named last changes fastest.
Arguments:
- heat: float32 [64, 256, 256], P('gz', ('groups', 'gx'), 'gy'), parts along dimension 1, may hold values from -6 to 6
- material: int32 [64, 256, 256], P('gz', ('groups', 'gx'), 'gy'), parts along dimension 1, may hold values from 0 to 7
- table: float32 [8], replicated, may hold values from 0.5 to 8
Outputs:
- temperature: float32 [64, 256, 256], P('gz', ('groups', 'gx'), 'gy'), parts along dimension 1
The draws below stay inside these ranges and needn't reach their ends.
There are 2 independent parts, one for each index of `groups`. The reference program is written for one: setup_inputs(seed, part) draws one part's arguments, and reference() takes and returns one part's arrays. A program takes and returns all parts, laid end to end along the dimension named above; an argument that names none is the same for every part. Nothing has to cross between parts.
All inputs are finite; a program needn't handle non-finite values.
Results may differ from the reference program's by a relative error of at most 0.0003.
Values sent between devices are 32-bit elements; how exact they have to be, the bound alone decides.
A program may use at most 64 MiB of HBM per device.

```python
import math
import jax
import jax.numpy as jnp
from jax import lax

NMAT = 8
BLOCK = 16
PRE = 2
POST = 2
NZ = 64
NX = 128
NY = 256
MZ = 4
MX = 8
MY = 16


def set_ends(values, own_key, low, high):
    longest = values.shape.index(max(values.shape))
    spots = []
    for shift in (0, 1):
        where = [jax.random.randint(jax.random.fold_in(own_key, axis), (), 0, length) for axis, length in enumerate(values.shape)]
        where[longest] = (where[longest] + shift) % values.shape[longest]
        spots.append(tuple(where))
    return values.at[spots[0]].set(low).at[spots[1]].set(high)


def block_scale(stream_key, shape, shards, least, high):
    def one(position, blocks):
        steps = jax.random.uniform(jax.random.fold_in(jax.random.fold_in(stream_key, 6), position), (blocks,), jnp.float32, least / len(shards), high / len(shards))
        return jnp.repeat(jnp.exp(steps), shape[position] // blocks).reshape((-1,) + (1,) * (len(shape) - position - 1))

    gain = one(*shards[0])
    for cut in shards[1:]:
        gain = gain * one(*cut)
    return gain


def noise(own_key, extent, width, limit, pieces=(), dtype=jnp.bfloat16):
    array = width * jax.random.normal(own_key, extent, jnp.float32)
    if pieces:
        array = array * block_scale(own_key, extent, pieces, -0.22, 0.18)
    return jnp.clip(array, -limit, limit).astype(dtype)


def setup_inputs(seed: int = 0, part: int = 0) -> dict:
    seeds = jax.random.split(jax.random.key(seed), 4)
    part_keys = jax.random.split(jax.random.fold_in(seeds[3], part), 4)
    heat = noise(part_keys[0], (NZ, NX, NY), 1.0, 6.0, ((0, 2), (1, 4), (2, 2)), jnp.float32)
    material = set_ends(jax.random.randint(part_keys[1], (NZ, NX, NY), 0, NMAT), jax.random.fold_in(part_keys[1], 1), 0, NMAT - 1).astype(jnp.int32)
    table = jnp.clip(jnp.exp(jax.random.uniform(seeds[2], (NMAT,), jnp.float32, math.log(0.5), math.log(8.0))), 0.5, 8.0)
    return dict(heat=heat, material=material, table=table)


def harmonic(center, other):
    inside = other > 0.0
    total = jnp.where(inside, center + other, 1.0)
    return jnp.where(inside, 2.0 * center * other / total, center)


def shifted(padded, dim, step, shape, margin):
    start = [margin, margin, margin]
    start[dim] = start[dim] + step
    return padded[start[0]:start[0] + shape[0], start[1]:start[1] + shape[1], start[2]:start[2] + shape[2]]


def stencil_weights(kpad, shape, margin):
    center = shifted(kpad, 0, 0, shape, margin)
    weights = []
    for dim in range(3):
        for step in (-1, 1):
            weights.append(harmonic(center, shifted(kpad, dim, step, shape, margin)))
    return weights


def neighbour_sum(weights, upad, shape, margin):
    total = None
    index = 0
    for dim in range(3):
        for step in (-1, 1):
            term = weights[index] * shifted(upad, dim, step, shape, margin)
            total = term if total is None else total + term
            index = index + 1
    return total


def sine_table(count):
    idx = jnp.arange(1, count + 1).astype(jnp.float32)
    return jnp.sin(math.pi * idx[:, None] * idx[None, :] / (count + 1))


def eigen_values(count):
    idx = jnp.arange(1, count + 1).astype(jnp.float32)
    return 2.0 - 2.0 * jnp.cos(math.pi * idx / (count + 1))


def coarse_solve(coarse, kbar):
    high = lax.Precision.HIGHEST
    sz, sx, sy = sine_table(MZ), sine_table(MX), sine_table(MY)
    hat = jnp.einsum('az,zxy->axy', sz, coarse, precision=high)
    hat = jnp.einsum('bx,axy->aby', sx, hat, precision=high)
    hat = jnp.einsum('cy,aby->abc', sy, hat, precision=high)
    denom = eigen_values(MZ)[:, None, None] + eigen_values(MX)[None, :, None] + eigen_values(MY)[None, None, :]
    hat = hat / denom
    hat = jnp.einsum('az,zxy->axy', sz, hat, precision=high)
    hat = jnp.einsum('bx,axy->aby', sx, hat, precision=high)
    hat = jnp.einsum('cy,aby->abc', sy, hat, precision=high)
    scale = BLOCK * BLOCK * 8.0 / ((MZ + 1) * (MX + 1) * (MY + 1) * kbar)
    return hat * scale


def reference(heat, material, table):
    shape = heat.shape
    kappa = jnp.zeros(shape, jnp.float32)
    for mat in range(NMAT):
        kappa = kappa + jnp.where(material == mat, table[mat], 0.0)
    weights = stencil_weights(jnp.pad(kappa, 1), shape, 1)
    diag = weights[0] + weights[1] + weights[2] + weights[3] + weights[4] + weights[5]
    parity = (lax.broadcasted_iota(jnp.int32, shape, 0) + lax.broadcasted_iota(jnp.int32, shape, 1)
              + lax.broadcasted_iota(jnp.int32, shape, 2)) % 2
    red = parity == 0
    black = parity == 1

    def sweep(field):
        for mask in (red, black):
            upad = jnp.pad(field, 1)
            field = jnp.where(mask, (heat + neighbour_sum(weights, upad, shape, 1)) / diag, field)
        return field

    field = jnp.zeros(shape, jnp.float32)
    for turn in range(PRE):
        field = sweep(field)
    upad = jnp.pad(field, 1)
    residual = heat - (diag * field - neighbour_sum(weights, upad, shape, 1))
    coarse = residual.reshape(MZ, BLOCK, MX, BLOCK, MY, BLOCK).mean(axis=(1, 3, 5))
    correction = coarse_solve(coarse, jnp.mean(table))
    fine = jnp.broadcast_to(correction[:, None, :, None, :, None], (MZ, BLOCK, MX, BLOCK, MY, BLOCK)).reshape(shape)
    field = field + fine
    for turn in range(POST):
        field = sweep(field)
    return field
```

```python
import functools
import math

import jax
import jax.numpy as jnp
import numpy as np
from jax import lax
from jax.experimental import pallas as pl
from jax.experimental.pallas import tpu as pltpu
from jax.sharding import PartitionSpec as P

BLOCK = 16
PAD = 8
MESH = pl.DeviceIdType.MESH
HIGH = lax.Precision.HIGHEST
ROUNDS = 8


def sine_rows(count):
    j = np.arange(-1, count + 1)[:, None] + 1.0
    k = np.arange(count)[None, :] + 1.0
    rows = np.sin(math.pi * j * k / (count + 1))
    rows[0] = 0.0
    rows[-1] = 0.0
    return rows


def tables(shape, n_gx, n_gy, n_gz):
    lz, lx, ly = (s // BLOCK for s in shape)
    fz, fx, fy = lz * n_gz, lx * n_gx, ly * n_gy
    cols = fz * fy
    wide = -(-cols // 128) * 128
    sz, sx, sy = sine_rows(fz), sine_rows(fx), sine_rows(fy)
    zs = np.arange(-1, shape[0] + 1)
    ys = np.arange(-1, shape[2] + 1)
    spread = np.zeros((n_gy, n_gz, wide, (lz + 4) * 128))
    gather = np.zeros((n_gy, n_gz, lz * 128, wide))
    for a in range(n_gy):
        yrow = np.floor_divide(ys + a * shape[2], BLOCK) + 1
        for b in range(n_gz):
            zrow = np.arange(-1, lz + 1) + b * lz + 1
            for i, row in enumerate(zrow):
                block = np.einsum("p,yq->pqy", sz[row], sy[yrow[1:-1]]).reshape(cols, -1)
                spread[a, b, :cols, i * 128 : i * 128 + shape[2]] = block
                if 1 <= i <= lz:
                    gather[a, b, (i - 1) * 128 : i * 128, :cols] = block.T
            fine = np.floor_divide(np.arange(shape[0]) + b * shape[0], BLOCK) + 1
            for side, row in ((0, yrow[0]), (1, yrow[-1])):
                block = np.einsum("zp,q->pqz", sz[fine], sy[row]).reshape(cols, -1)
                at = (lz + 2 + side) * 128
                spread[a, b, :cols, at : at + shape[0]] = block
    rows = shape[1] + 2 * PAD
    expand = np.zeros((n_gx, rows, fx))
    shrink = np.zeros((n_gx, fx, shape[1]))
    for a in range(n_gx):
        xs = np.arange(-1, shape[1] + 1) + a * shape[1]
        block = sx[np.floor_divide(xs, BLOCK) + 1]
        expand[a, PAD - 1 : PAD + shape[1] + 1] = block
        shrink[a] = block[1:-1].T
    lam = lambda n: 2.0 - 2.0 * np.cos(math.pi * (np.arange(n) + 1.0) / (n + 1))
    total = lam(fx)[:, None] + (lam(fz)[:, None] + lam(fy)[None, :]).reshape(1, -1)
    scale = np.zeros((fx, wide))
    scale[:, :cols] = BLOCK * BLOCK * 8.0 / ((fz + 1) * (fx + 1) * (fy + 1)) / total / BLOCK**3
    return [t.astype(np.float32) for t in (spread, gather, expand, shrink, scale)]


def kernel(
    sizes, shape, heat, mat, table, spread_hbm, gather_hbm, expand_hbm, shrink_hbm, scale,
    out, kp, u, wd, hd, dg, vsum, corr, spread, gather, expand, shrink,
    s_z, r_z, s_x, r_x, s_y, r_y, got, tab_sem, send_sem, recv_sem, gsend, grecv,
):
    n_gx, n_gy, n_gz = sizes
    nz, nx, ny = shape
    lz = nz // BLOCK
    rows = nx + 2 * PAD
    gx, gy, gz = lax.axis_index("gx"), lax.axis_index("gy"), lax.axis_index("gz")
    count = n_gx * n_gy * n_gz
    me = (gx * n_gy + gy) * n_gz + gz

    def peer_of(step):
        other = lax.rem(me + step, count)
        return other, {
            "gx": other // (n_gy * n_gz),
            "gy": lax.rem(other // n_gz, n_gy),
            "gz": lax.rem(other, n_gz),
        }

    barrier = pltpu.get_barrier_semaphore()

    def greet(step, carry):
        _, where = peer_of(step)
        pl.semaphore_signal(barrier, inc=1, device_id=where, device_id_type=MESH)
        return carry

    lax.fori_loop(1, count, greet, 0)

    fetch = [
        pltpu.make_async_copy(spread_hbm.at[gy, gz], spread, tab_sem.at[0]),
        pltpu.make_async_copy(gather_hbm.at[gy, gz], gather, tab_sem.at[1]),
        pltpu.make_async_copy(expand_hbm.at[gx], expand, tab_sem.at[2]),
        pltpu.make_async_copy(shrink_hbm.at[gx], shrink, tab_sem.at[3]),
    ]
    for copy in fetch:
        copy.start()

    faces = []
    for bufs, name, index, size, sem in (
        ((s_z, r_z), "gz", gz, n_gz, 0),
        ((s_x, r_x), "gx", gx, n_gx, 2),
    ):
        if size > 1:
            faces.append((*bufs, 0, 1, index > 0, {name: index - 1}, sem))
            faces.append((*bufs, 1, 0, index < size - 1, {name: index + 1}, sem + 1))
    single = n_gy == 2
    if single:
        edge = (ny - 1) * (1 - gy)
        edges = [edge]
        faces.append((s_y, r_y, 0, 0, None, {"gy": 1 - gy}, 4))
    else:
        edges = [0, ny - 1]
        if n_gy > 1:
            faces.append((s_y, r_y, 0, 1, gy > 0, {"gy": gy - 1}, 4))
            faces.append((s_y, r_y, 1, 0, gy < n_gy - 1, {"gy": gy + 1}, 5))

    def copies(turn, landing):
        for src, dst, mine, theirs, exists, where, sem in faces:
            there = sem if single and sem == 4 else (sem // 2) * 2 + theirs
            yield exists, pltpu.make_async_remote_copy(
                src_ref=src.at[turn, mine],
                dst_ref=dst.at[turn, mine if landing else theirs],
                send_sem=send_sem.at[turn, sem],
                recv_sem=recv_sem.at[turn, sem if landing else there],
                device_id=where,
                device_id_type=MESH,
            )

    def guarded(exists, action):
        if exists is None:
            action()
        else:
            pl.when(exists)(action)

    lane = lax.broadcasted_iota(jnp.int32, (nx, ny), 1)
    row = lax.broadcasted_iota(jnp.int32, (nx, ny), 0)
    odd = lax.rem(lane + row, 2)
    zero = jnp.zeros((nx, ny), jnp.float32)
    for buf, size, index in ((r_z, n_gz, gz), (r_x, n_gx, gx), (r_y, n_gy, gy)):
        if buf is r_y and single:
            continue
        for side, at in ((0, 0), (1, size - 1)):
            def clear(buf=buf, side=side):
                for turn in range(ROUNDS):
                    buf[turn, side] = jnp.zeros(buf.shape[2:], jnp.float32)

            pl.when(index == at)(clear)

    def slab(z):
        return pl.ds(pl.multiple_of(z * rows, 8) + PAD, nx)

    def packed(packs, value, z):
        result = []
        for pack, at in zip(packs, edges):
            turned = pltpu.roll(value, lax.rem(z - at + ny, ny), 1)
            result.append(jnp.where(lane == z, turned, pack))
        return tuple(result)

    blank = tuple(zero for _ in edges)

    def send(turn, field, packs):
        s_z[turn, 0] = field[pl.ds(rows + PAD, nx), :]
        s_z[turn, 1] = field[pl.ds(nz * rows + PAD, nx), :]
        for side, at in ((0, PAD), (1, PAD + nx - 1)):
            s_x[turn, side] = field[pl.ds(rows + at, nz, stride=rows), :]
        for side, pack in enumerate(packs):
            s_y[turn, side] = pack
        for exists, copy in copies(turn, False):
            guarded(exists, copy.start)

    def receive(turn, field):
        for exists, copy in copies(turn, True):
            guarded(exists, copy.wait_recv)
        field[pl.ds(PAD, nx), :] = r_z[turn, 0]
        field[pl.ds((nz + 1) * rows + PAD, nx), :] = r_z[turn, 1]
        for side, at in ((0, PAD - 1), (1, PAD + nx)):
            field[pl.ds(rows + at, nz, stride=rows), :] = r_x[turn, side]

    def beside(value, halos, z, strict):
        low, high = pltpu.roll(value, 1, 1), pltpu.roll(value, ny - 1, 1)
        if single:
            halo = pltpu.roll(halos[0], lax.rem(edge - z + ny, ny), 1)
            if strict:
                outer = gy.astype(jnp.float32)
                return (
                    jnp.where(lane == 0, halo * outer, low),
                    jnp.where(lane == ny - 1, halo * (1.0 - outer), high),
                )
            return jnp.where(lane == 0, halo, low), jnp.where(lane == ny - 1, halo, high)
        if n_gy == 1:
            return jnp.where(lane == 0, 0.0, low), jnp.where(lane == ny - 1, 0.0, high)
        first = pltpu.roll(halos[0], lax.rem(ny - z, ny), 1)
        last = pltpu.roll(halos[1], lax.rem(2 * ny - 1 - z, ny), 1)
        return jnp.where(lane == 0, first, low), jnp.where(lane == ny - 1, last, high)

    def around(field, halos, z, strict=False):
        value = field[slab(z + 1), :]
        low, high = beside(value, halos, z, strict)
        at = pl.multiple_of((z + 1) * rows, 8) + PAD
        return value, (
            field[slab(z), :],
            field[slab(z + 2), :],
            field[pl.ds(at - 1, nx), :],
            field[pl.ds(at + 1, nx), :],
            low,
            high,
        )

    def y_halos(turn):
        return [r_y[turn, side] for side in range(len(edges))]

    def conduct(z, packs):
        ids = mat[z]
        value = jnp.full((nx, ny), table[0], jnp.float32)
        for m in range(1, table.shape[0]):
            value = jnp.where(ids == m, table[m], value)
        kp[slab(z + 1), :] = value
        return packed(packs, value, z)

    packs = lax.fori_loop(0, nz, conduct, blank, unroll=2)
    pl.semaphore_wait(barrier, count - 1)
    send(0, kp, packs)
    receive(0, kp)
    halos = y_halos(0)

    def weigh(z, packs):
        center, others = around(kp, halos, z, True)
        diag = None
        inner = []
        for other in others:
            inside = other > 0.0
            weight = 2.0 * center * other / (center + other)
            full = jnp.where(inside, weight, center)
            inner.append(jnp.where(inside, weight, 0.0))
            diag = full if diag is None else diag + full
        inverse = 1.0 / diag
        for face in range(6):
            wd[face, z] = inner[face] * inverse
        ratio = heat[z] * inverse
        hd[z] = ratio
        dg[z] = diag
        value = jnp.where(odd == lax.rem(z, 2), ratio, 0.0)
        u[slab(z + 1), :] = value
        return packed(packs, value, z)

    packs = lax.fori_loop(0, nz, weigh, blank)
    send(1, u, packs)

    def total(z, halos):
        value, others = around(u, halos, z)
        result = hd[z]
        for face in range(6):
            result = result + wd[face, z] * others[face]
        return value, result

    def half(color, halos, last=False):
        def step(z, packs):
            value, result = total(z, halos)
            value = jnp.where(odd == lax.rem(z + color, 2), result, value)
            if last:
                out[z] = value
                return packs
            u[slab(z + 1), :] = value
            return packed(packs, value, z)

        return lax.fori_loop(0, nz, step, blank, unroll=2)

    for turn, color in ((2, 1), (3, 0), (4, 1)):
        receive(turn - 1, u)
        packs = half(color, y_halos(turn - 1))
        send(turn, u, packs)
    receive(4, u)
    halos = y_halos(4)

    for layer in range(lz):
        def gap(z, acc):
            value, result = total(z, halos)
            return acc + jnp.where(odd == lax.rem(z, 2), dg[z] * (result - value), 0.0)

        vsum[:, layer * ny : (layer + 1) * ny] = lax.fori_loop(
            layer * BLOCK, (layer + 1) * BLOCK, gap, zero, unroll=2
        )
    for copy in fetch:
        copy.wait()
    part = jnp.dot(shrink[...], vsum[...], precision=HIGH, preferred_element_type=jnp.float32)
    part = jnp.dot(part, gather[...], precision=HIGH, preferred_element_type=jnp.float32)
    got[me] = part

    def gathering(step, start):
        other, where = peer_of(step)
        copy = pltpu.make_async_remote_copy(
            src_ref=got.at[me],
            dst_ref=got.at[me if start else other],
            send_sem=gsend.at[step],
            recv_sem=grecv.at[me if start else other],
            device_id=where,
            device_id_type=MESH,
        )
        return copy

    def give(step, carry):
        gathering(step, True).start()
        return carry

    def take(step, carry):
        gathering(step, False).wait_recv()
        return carry

    lax.fori_loop(1, count, give, 0)
    lax.fori_loop(1, count, take, 0)
    if count <= 32:
        hat = got[0]
        for i in range(1, count):
            hat = hat + got[i]
    else:
        hat = lax.fori_loop(1, count, lambda i, acc: acc + got[i], got[0])
    kbar = table[0]
    for m in range(1, table.shape[0]):
        kbar = kbar + table[m]
    kbar = kbar / table.shape[0]
    hat = hat * scale[...] / kbar
    hat = jnp.dot(hat, spread[...], precision=HIGH, preferred_element_type=jnp.float32)
    corr[...] = jnp.dot(expand[...], hat, precision=HIGH, preferred_element_type=jnp.float32)

    def correct(z, carry):
        layer = (z + BLOCK - 1) // BLOCK
        at = pl.ds(pl.multiple_of(z * rows, 8), rows)
        u[at, :] = u[at, :] + corr[:, pl.ds(pl.multiple_of(layer * ny, ny), ny)]
        return carry

    lax.fori_loop(0, nz + 2, correct, 0, unroll=2)
    sides = [corr[PAD : PAD + nx, (lz + 2 + s) * ny : (lz + 3 + s) * ny] for s in range(2)]
    if single:
        upper = gy.astype(jnp.float32)
        halos = [halos[0] + sides[0] * upper + sides[1] * (1.0 - upper)]
    else:
        halos = [halo + side for halo, side in zip(halos, sides)]

    packs = half(0, halos)
    send(5, u, packs)
    for turn, color in ((6, 1), (7, 0)):
        receive(turn - 1, u)
        packs = half(color, y_halos(turn - 1))
        send(turn, u, packs)
    receive(7, u)
    half(1, y_halos(7), True)

    for turn in range(ROUNDS):
        for exists, copy in copies(turn, False):
            guarded(exists, copy.wait_send)

    def sent(step, carry):
        gathering(step, True).wait_send()
        return carry

    lax.fori_loop(1, count, sent, 0)


def per_device(sizes, heat, material, table):
    shape = heat.shape
    nz, nx, ny = shape
    n_gx, n_gy, n_gz = sizes
    consts = tables(shape, *sizes)
    spread, gather, expand, shrink, scale = consts
    count = n_gx * n_gy * n_gz
    rows = nx + 2 * PAD
    sides = 1 if n_gy == 2 else 2
    f32 = jnp.float32
    vmem = pl.BlockSpec(memory_space=pltpu.VMEM)
    hbm = pl.BlockSpec(memory_space=pl.ANY)
    faces = [
        pltpu.VMEM((ROUNDS, 2, nx, ny), f32),
        pltpu.VMEM((ROUNDS, 2, nx, ny), f32),
        pltpu.VMEM((ROUNDS, 2, nz, ny), f32),
        pltpu.VMEM((ROUNDS, 2, nz, ny), f32),
        pltpu.VMEM((ROUNDS, sides, nx, ny), f32),
        pltpu.VMEM((ROUNDS, sides, nx, ny), f32),
    ]
    return pl.pallas_call(
        functools.partial(kernel, sizes, shape),
        out_shape=jax.ShapeDtypeStruct(shape, f32),
        in_specs=[vmem, vmem, pl.BlockSpec(memory_space=pltpu.SMEM), hbm, hbm, hbm, hbm, vmem],
        out_specs=vmem,
        scratch_shapes=[
            pltpu.VMEM(((nz + 2) * rows, ny), f32),
            pltpu.VMEM(((nz + 2) * rows, ny), f32),
            pltpu.VMEM((6, nz, nx, ny), f32),
            pltpu.VMEM(shape, f32),
            pltpu.VMEM(shape, f32),
            pltpu.VMEM((nx, nz // BLOCK * ny), f32),
            pltpu.VMEM((rows, spread.shape[3]), f32),
            pltpu.VMEM(spread.shape[2:], f32),
            pltpu.VMEM(gather.shape[2:], f32),
            pltpu.VMEM(expand.shape[1:], f32),
            pltpu.VMEM(shrink.shape[1:], f32),
            *faces,
            pltpu.VMEM((count, *scale.shape), f32),
            pltpu.SemaphoreType.DMA((4,)),
            pltpu.SemaphoreType.DMA((ROUNDS, 6)),
            pltpu.SemaphoreType.DMA((ROUNDS, 6)),
            pltpu.SemaphoreType.DMA((count,)),
            pltpu.SemaphoreType.DMA((count,)),
        ],
        compiler_params=pltpu.CompilerParams(
            collective_id=0, has_side_effects=True, vmem_limit_bytes=50 * 1024 * 1024
        ),
    )(heat, material, table, *(jnp.asarray(c) for c in consts))


def solution(mesh):
    sizes = (mesh.shape["gx"], mesh.shape["gy"], mesh.shape["gz"])
    spec = P("gz", ("groups", "gx"), "gy")
    return jax.shard_map(
        functools.partial(per_device, sizes),
        mesh=mesh,
        in_specs=(spec, spec, P()),
        out_specs=spec,
        check_vma=False,
    )
```

```python
import functools
import math

import jax
import jax.numpy as jnp
import numpy as np
from jax import lax
from jax.experimental import pallas as pl
from jax.experimental.pallas import tpu as pltpu
from jax.sharding import PartitionSpec as P

BLOCK = 16
PAD = 8
UNROLL = 4
MESH = pl.DeviceIdType.MESH
HIGH = lax.Precision.HIGHEST
ROUNDS = 9


def sine_rows(count):
    j = np.arange(-1, count + 1)[:, None] + 1.0
    k = np.arange(count)[None, :] + 1.0
    rows = np.sin(math.pi * j * k / (count + 1))
    rows[0] = 0.0
    rows[-1] = 0.0
    return rows


def tables(shape, n_gx, n_gy, n_gz):
    lz, lx, ly = (s // BLOCK for s in shape)
    fz, fx, fy = lz * n_gz, lx * n_gx, ly * n_gy
    cols = fz * fy
    wide = -(-cols // 128) * 128
    sz, sx, sy = sine_rows(fz), sine_rows(fx), sine_rows(fy)
    zs = np.arange(-1, shape[0] + 1)
    ys = np.arange(-1, shape[2] + 1)
    spread = np.zeros((n_gy, n_gz, wide, (lz + 4) * 128))
    gather = np.zeros((n_gy, n_gz, lz * 128, wide))
    for a in range(n_gy):
        yrow = np.floor_divide(ys + a * shape[2], BLOCK) + 1
        for b in range(n_gz):
            zrow = np.arange(-1, lz + 1) + b * lz + 1
            for i, row in enumerate(zrow):
                block = np.einsum("p,yq->pqy", sz[row], sy[yrow[1:-1]]).reshape(cols, -1)
                spread[a, b, :cols, i * 128 : i * 128 + shape[2]] = block
                if 1 <= i <= lz:
                    gather[a, b, (i - 1) * 128 : i * 128, :cols] = block.T
            fine = np.floor_divide(np.arange(0, shape[0], 2) + b * shape[0], BLOCK) + 1
            for side, row in ((0, yrow[0]), (1, yrow[-1])):
                block = np.einsum("zp,q->pqz", sz[fine], sy[row]).reshape(cols, -1)
                at = (lz + 2 + side) * 128
                spread[a, b, :cols, at : at + shape[0] // 2] = block
    rows = shape[1] + 2 * PAD
    expand = np.zeros((n_gx, rows, fx))
    shrink = np.zeros((n_gx, fx, shape[1]))
    for a in range(n_gx):
        xs = np.arange(-1, shape[1] + 1) + a * shape[1]
        block = sx[np.floor_divide(xs, BLOCK) + 1]
        expand[a, PAD - 1 : PAD + shape[1] + 1] = block
        shrink[a] = block[1:-1].T
    lam = lambda n: 2.0 - 2.0 * np.cos(math.pi * (np.arange(n) + 1.0) / (n + 1))
    total = lam(fx)[:, None] + (lam(fz)[:, None] + lam(fy)[None, :]).reshape(1, -1)
    scale = np.zeros((fx, wide))
    scale[:, :cols] = BLOCK * BLOCK * 8.0 / ((fz + 1) * (fx + 1) * (fy + 1)) / total / BLOCK**3
    return [t.astype(np.float32) for t in (spread, gather, expand, shrink, scale)]


def kernel(
    sizes, shape, heat_hbm, mat_hbm, table_hbm, spread_hbm, gather_hbm, expand_hbm, shrink_hbm, scale_hbm,
    out, heat, mat, table, kr, kb, red, black, wd, hd, dg, vsum, corr, spread, gather, expand, shrink,
    scale, s_z, r_z, s_x, r_x, s_y, r_y, got, tab_sem, send_sem, recv_sem, gsend, grecv,
):
    n_gx, n_gy, n_gz = sizes
    nz, nx, ny = shape
    lz = nz // BLOCK
    pairs = nz // 2
    rows = nx + 2 * PAD
    gx, gy, gz = lax.axis_index("gx"), lax.axis_index("gy"), lax.axis_index("gz")
    count = n_gx * n_gy * n_gz
    me = (gx * n_gy + gy) * n_gz + gz

    def peer_of(step):
        other = lax.rem(me + step, count)
        return other, {
            "gx": other // (n_gy * n_gz),
            "gy": lax.rem(other // n_gz, n_gy),
            "gz": lax.rem(other, n_gz),
        }

    inputs = [
        pltpu.make_async_copy(table_hbm, table, tab_sem.at[5]),
        pltpu.make_async_copy(mat_hbm, mat, tab_sem.at[6]),
        pltpu.make_async_copy(heat_hbm, heat, tab_sem.at[7]),
    ]
    for copy in inputs:
        copy.start()
    barrier = pltpu.get_barrier_semaphore()

    def greet(step, carry):
        _, where = peer_of(step)
        pl.semaphore_signal(barrier, inc=1, device_id=where, device_id_type=MESH)
        return carry

    lax.fori_loop(1, count, greet, 0)

    fetch = [
        pltpu.make_async_copy(spread_hbm.at[gy, gz], spread, tab_sem.at[0]),
        pltpu.make_async_copy(gather_hbm.at[gy, gz], gather, tab_sem.at[1]),
        pltpu.make_async_copy(expand_hbm.at[gx], expand, tab_sem.at[2]),
        pltpu.make_async_copy(shrink_hbm.at[gx], shrink, tab_sem.at[3]),
        pltpu.make_async_copy(scale_hbm, scale, tab_sem.at[4]),
    ]
    for copy in fetch:
        copy.start()

    faces = []
    for bufs, name, index, size, sem in (
        ((s_z, r_z), "gz", gz, n_gz, 0),
        ((s_x, r_x), "gx", gx, n_gx, 2),
    ):
        if size > 1:
            faces.append((*bufs, 0, 1, index > 0, {name: index - 1}, sem))
            faces.append((*bufs, 1, 0, index < size - 1, {name: index + 1}, sem + 1))
    single = n_gy == 2
    if single:
        edge = (ny - 1) * (1 - gy)
        edges = [edge]
        faces.append((s_y, r_y, 0, 0, None, {"gy": 1 - gy}, 4))
    else:
        edges = [0, ny - 1]
        if n_gy > 1:
            faces.append((s_y, r_y, 0, 1, gy > 0, {"gy": gy - 1}, 4))
            faces.append((s_y, r_y, 1, 0, gy < n_gy - 1, {"gy": gy + 1}, 5))

    def copies(turn, landing):
        for src, dst, mine, theirs, exists, where, sem in faces:
            there = sem if single and sem == 4 else (sem // 2) * 2 + theirs
            yield exists, pltpu.make_async_remote_copy(
                src_ref=src.at[turn, mine],
                dst_ref=dst.at[turn, mine if landing else theirs],
                send_sem=send_sem.at[turn, sem],
                recv_sem=recv_sem.at[turn, sem if landing else there],
                device_id=where,
                device_id_type=MESH,
            )

    def guarded(exists, action):
        if exists is None:
            action()
        else:
            pl.when(exists)(action)

    lane = lax.broadcasted_iota(jnp.int32, (nx, ny), 1)
    row = lax.broadcasted_iota(jnp.int32, (nx, ny), 0)
    even = lax.rem(lane + row, 2) == 0
    zero = jnp.zeros((nx, ny), jnp.float32)
    for buf, size, index in ((r_z, n_gz, gz), (r_x, n_gx, gx), (r_y, n_gy, gy)):
        if buf is r_y and single:
            continue
        for side, at in ((0, 0), (1, size - 1)):
            def clear(buf=buf, side=side):
                for turn in range(ROUNDS):
                    buf[turn, side] = jnp.zeros(buf.shape[2:], jnp.float32)

            pl.when(index == at)(clear)

    def slab(z):
        return pl.ds(pl.multiple_of(z * rows, 8) + PAD, nx)

    def packed(packs, value, z):
        result = []
        for pack, at in zip(packs, edges):
            turned = pltpu.roll(value, lax.rem(z - at + ny, ny), 1)
            result.append(jnp.where(lane == z, turned, pack))
        return tuple(result)

    blank = tuple(zero for _ in edges)

    def send(turn, field, packs):
        s_z[turn, 0] = field[pl.ds(rows + PAD, nx), :]
        s_z[turn, 1] = field[pl.ds(pairs * rows + PAD, nx), :]
        for side, at in ((0, PAD), (1, PAD + nx - 1)):
            s_x[turn, side] = field[pl.ds(rows + at, pairs, stride=rows), :]
        for side, pack in enumerate(packs):
            s_y[turn, side] = pack
        for exists, copy in copies(turn, False):
            guarded(exists, copy.start)

    def receive(turn, field):
        for exists, copy in copies(turn, True):
            guarded(exists, copy.wait_recv)
        field[pl.ds(PAD, nx), :] = r_z[turn, 0]
        field[pl.ds((pairs + 1) * rows + PAD, nx), :] = r_z[turn, 1]
        for side, at in ((0, PAD - 1), (1, PAD + nx)):
            field[pl.ds(rows + at, pairs, stride=rows), :] = r_x[turn, side]

    def beside(value, halos, z, strict):
        low, high = pltpu.roll(value, 1, 1), pltpu.roll(value, ny - 1, 1)
        if single:
            halo = pltpu.roll(halos[0], lax.rem(edge - z + ny, ny), 1)
            if strict:
                outer = gy.astype(jnp.float32)
                return (
                    jnp.where(lane == 0, halo * outer, low),
                    jnp.where(lane == ny - 1, halo * (1.0 - outer), high),
                )
            return jnp.where(lane == 0, halo, low), jnp.where(lane == ny - 1, halo, high)
        if n_gy == 1:
            return jnp.where(lane == 0, 0.0, low), jnp.where(lane == ny - 1, 0.0, high)
        first = pltpu.roll(halos[0], lax.rem(ny - z, ny), 1)
        last = pltpu.roll(halos[1], lax.rem(2 * ny - 1 - z, ny), 1)
        return jnp.where(lane == 0, first, low), jnp.where(lane == ny - 1, last, high)

    def around(field, color, halos, z, strict=False):
        same = field[slab(z + 1), :]
        before, after = field[slab(z), :], field[slab(z + 2), :]
        low, high = beside(same, halos, z, strict)
        at = pl.multiple_of((z + 1) * rows, 8) + PAD
        return (
            same,
            jnp.where(even, before, after) if color == 0 else jnp.where(even, after, before),
            field[pl.ds(at - 1, nx), :],
            field[pl.ds(at + 1, nx), :],
            low,
            high,
        )

    def y_halos(turn):
        return [r_y[turn, side] for side in range(len(edges))]

    def loop(count, step, carry, start=0):
        return lax.fori_loop(start, count, step, carry, unroll=UNROLL)

    def conduct(z, packs):
        values = []
        for layer in range(2):
            ids = mat[2 * z + layer]
            value = jnp.full((nx, ny), table[0], jnp.float32)
            for m in range(1, table.shape[0]):
                value = jnp.where(ids == m, table[m], value)
            values.append(value)
        first = jnp.where(even, values[0], values[1])
        second = jnp.where(even, values[1], values[0])
        kr[slab(z + 1), :] = first
        kb[slab(z + 1), :] = second
        return packed(packs[0], first, z), packed(packs[1], second, z)

    inputs[0].wait()
    inputs[1].wait()
    packs = loop(pairs, conduct, (blank, blank))
    pl.semaphore_wait(barrier, count - 1)
    send(0, kr, packs[0])
    send(1, kb, packs[1])
    inputs[2].wait()
    receive(0, kr)
    receive(1, kb)

    def weigh(color, own, field, turn, first):
        halos = y_halos(turn)

        def step(z, packs):
            center = own[slab(z + 1), :]
            others = around(field, color, halos, z, True)
            diag = None
            inner = []
            for other in others:
                inside = other > 0.0
                weight = 2.0 * center * other / (center + other)
                full = jnp.where(inside, weight, center)
                inner.append(jnp.where(inside, weight, 0.0))
                diag = full if diag is None else diag + full
            inverse = 1.0 / diag
            for face in range(6):
                wd[color, face, z] = inner[face] * inverse
            lower, upper = heat[2 * z], heat[2 * z + 1]
            source = jnp.where(even, lower, upper) if color == 0 else jnp.where(even, upper, lower)
            ratio = source * inverse
            hd[color, z] = ratio
            if not first:
                return packs
            dg[z] = diag
            red[slab(z + 1), :] = ratio
            return packed(packs, ratio, z)

        return loop(pairs, step, blank if first else 0)

    packs = weigh(0, kr, kb, 1, True)
    send(2, red, packs)
    weigh(1, kb, kr, 0, False)

    def total(color, field, halos, z):
        others = around(field, color, halos, z)
        result = hd[color, z]
        for face in range(6):
            result = result + wd[color, face, z] * others[face]
        return result

    def half(color, halos):
        field, own = ((black, red), (red, black))[color]

        def step(z, packs):
            value = total(color, field, halos, z)
            own[slab(z + 1), :] = value
            return packed(packs, value, z)

        return loop(pairs, step, blank)

    for turn, color in ((3, 1), (4, 0), (5, 1)):
        receive(turn - 1, (black, red)[color])
        packs = half(color, y_halos(turn - 1))
        send(turn, (red, black)[color], packs)
    receive(5, black)
    halos = y_halos(5)

    for layer in range(lz):
        def gap(z, acc):
            return acc + dg[z] * (total(0, black, halos, z) - red[slab(z + 1), :])

        vsum[:, layer * ny : (layer + 1) * ny] = loop(
            (layer + 1) * BLOCK // 2, gap, zero, layer * BLOCK // 2
        )
    for copy in fetch:
        copy.wait()
    part = jnp.dot(shrink[...], vsum[...], precision=HIGH, preferred_element_type=jnp.float32)
    part = jnp.dot(part, gather[...], precision=HIGH, preferred_element_type=jnp.float32)
    got[me] = part

    def gathering(step, start):
        other, where = peer_of(step)
        copy = pltpu.make_async_remote_copy(
            src_ref=got.at[me],
            dst_ref=got.at[me if start else other],
            send_sem=gsend.at[step],
            recv_sem=grecv.at[me if start else other],
            device_id=where,
            device_id_type=MESH,
        )
        return copy

    def give(step, carry):
        gathering(step, True).start()
        return carry

    def take(step, carry):
        gathering(step, False).wait_recv()
        return carry

    lax.fori_loop(1, count, give, 0)
    lax.fori_loop(1, count, take, 0)
    if count <= 32:
        hat = got[0]
        for i in range(1, count):
            hat = hat + got[i]
    else:
        hat = lax.fori_loop(1, count, lambda i, acc: acc + got[i], got[0])
    kbar = table[0]
    for m in range(1, table.shape[0]):
        kbar = kbar + table[m]
    kbar = kbar / table.shape[0]
    hat = hat * scale[...] / kbar
    hat = jnp.dot(hat, spread[...], precision=HIGH, preferred_element_type=jnp.float32)
    corr[...] = jnp.dot(expand[...], hat, precision=HIGH, preferred_element_type=jnp.float32)

    def correct(z, carry):
        layer = (z + BLOCK // 2 - 1) // (BLOCK // 2)
        at = pl.ds(pl.multiple_of(z * rows, 8), rows)
        black[at, :] = black[at, :] + corr[:, pl.ds(pl.multiple_of(layer * ny, ny), ny)]
        return carry

    lax.fori_loop(0, pairs + 2, correct, 0, unroll=2)
    sides = [corr[PAD : PAD + nx, (lz + 2 + s) * ny : (lz + 3 + s) * ny] for s in range(2)]
    if single:
        upper = gy.astype(jnp.float32)
        halos = [halos[0] + sides[0] * upper + sides[1] * (1.0 - upper)]
    else:
        halos = [halo + side for halo, side in zip(halos, sides)]

    packs = half(0, halos)
    send(6, red, packs)
    for turn, color in ((7, 1), (8, 0)):
        receive(turn - 1, (black, red)[color])
        packs = half(color, y_halos(turn - 1))
        send(turn, (red, black)[color], packs)
    receive(8, red)
    halos = y_halos(8)

    def finish(z, carry):
        last = total(1, red, halos, z)
        own = red[slab(z + 1), :]
        out[2 * z] = jnp.where(even, own, last)
        out[2 * z + 1] = jnp.where(even, last, own)
        return carry

    loop(pairs, finish, 0)

    for turn in range(ROUNDS):
        for exists, copy in copies(turn, False):
            guarded(exists, copy.wait_send)

    def sent(step, carry):
        gathering(step, True).wait_send()
        return carry

    lax.fori_loop(1, count, sent, 0)


def per_device(sizes, heat, material, table):
    shape = heat.shape
    nz, nx, ny = shape
    n_gx, n_gy, n_gz = sizes
    consts = tables(shape, *sizes)
    spread, gather, expand, shrink, scale = consts
    count = n_gx * n_gy * n_gz
    rows = nx + 2 * PAD
    sides = 1 if n_gy == 2 else 2
    f32 = jnp.float32
    vmem = pl.BlockSpec(memory_space=pltpu.VMEM)
    hbm = pl.BlockSpec(memory_space=pltpu.HBM)
    faces = [
        pltpu.VMEM((ROUNDS, 2, nx, ny), f32),
        pltpu.VMEM((ROUNDS, 2, nx, ny), f32),
        pltpu.VMEM((ROUNDS, 2, nz // 2, ny), f32),
        pltpu.VMEM((ROUNDS, 2, nz // 2, ny), f32),
        pltpu.VMEM((ROUNDS, sides, nx, ny), f32),
        pltpu.VMEM((ROUNDS, sides, nx, ny), f32),
    ]
    return pl.pallas_call(
        functools.partial(kernel, sizes, shape),
        out_shape=jax.ShapeDtypeStruct(shape, f32),
        in_specs=[hbm] * 8,
        out_specs=vmem,
        scratch_shapes=[
            pltpu.VMEM(shape, f32),
            pltpu.VMEM(shape, jnp.int32),
            pltpu.SMEM(table.shape, f32),
            *[pltpu.VMEM(((nz // 2 + 2) * rows, ny), f32)] * 4,
            pltpu.VMEM((2, 6, nz // 2, nx, ny), f32),
            pltpu.VMEM((2, nz // 2, nx, ny), f32),
            pltpu.VMEM((nz // 2, nx, ny), f32),
            pltpu.VMEM((nx, nz // BLOCK * ny), f32),
            pltpu.VMEM((rows, spread.shape[3]), f32),
            pltpu.VMEM(spread.shape[2:], f32),
            pltpu.VMEM(gather.shape[2:], f32),
            pltpu.VMEM(expand.shape[1:], f32),
            pltpu.VMEM(shrink.shape[1:], f32),
            pltpu.VMEM(scale.shape, f32),
            *faces,
            pltpu.VMEM((count, *scale.shape), f32),
            pltpu.SemaphoreType.DMA((8,)),
            pltpu.SemaphoreType.DMA((ROUNDS, 6)),
            pltpu.SemaphoreType.DMA((ROUNDS, 6)),
            pltpu.SemaphoreType.DMA((count,)),
            pltpu.SemaphoreType.DMA((count,)),
        ],
        compiler_params=pltpu.CompilerParams(
            collective_id=0, has_side_effects=True, vmem_limit_bytes=64 * 1024 * 1024
        ),
    )(heat, material, table, *(jnp.asarray(c) for c in consts))


def solution(mesh):
    sizes = (mesh.shape["gx"], mesh.shape["gy"], mesh.shape["gz"])
    spec = P("gz", ("groups", "gx"), "gy")
    return jax.shard_map(
        functools.partial(per_device, sizes),
        mesh=mesh,
        in_specs=(spec, spec, P()),
        out_specs=spec,
        check_vma=False,
    )
```

```python
import functools
import math

import jax
import jax.numpy as jnp
import numpy as np
from jax import lax
from jax.experimental import pallas as pl
from jax.experimental.pallas import tpu as pltpu
from jax.sharding import PartitionSpec as P

BLOCK = 16
PAD = 8
UNROLL = 8
MESH = pl.DeviceIdType.MESH
HIGH = lax.Precision.HIGHEST
ROUNDS = 9


def sine_rows(count):
    j = np.arange(-1, count + 1)[:, None] + 1.0
    k = np.arange(count)[None, :] + 1.0
    rows = np.sin(math.pi * j * k / (count + 1))
    rows[0] = 0.0
    rows[-1] = 0.0
    return rows


def tables(shape, n_gx, n_gy, n_gz):
    lz, lx, ly = (s // BLOCK for s in shape)
    fz, fx, fy = lz * n_gz, lx * n_gx, ly * n_gy
    cols = fz * fy
    wide = -(-cols // 128) * 128
    sz, sx, sy = sine_rows(fz), sine_rows(fx), sine_rows(fy)
    zs = np.arange(-1, shape[0] + 1)
    ys = np.arange(-1, shape[2] + 1)
    spread = np.zeros((n_gy, n_gz, wide, (lz + 4) * 128))
    gather = np.zeros((n_gy, n_gz, (2 * lz + 2) * 128, wide))
    for a in range(n_gy):
        yrow = np.floor_divide(ys + a * shape[2], BLOCK) + 1
        for b in range(n_gz):
            zrow = np.arange(-1, lz + 1) + b * lz + 1
            for i, row in enumerate(zrow):
                block = np.einsum("p,yq->pqy", sz[row], sy[yrow[1:-1]]).reshape(cols, -1)
                spread[a, b, :cols, i * 128 : i * 128 + shape[2]] = block
                gather[a, b, i * 128 : i * 128 + shape[2], :cols] = block.T
                if 1 <= i <= lz:
                    at = (lz + 1 + i) * 128
                    gather[a, b, at, :cols] = np.outer(sz[row], sy[yrow[0]]).reshape(-1)
                    gather[a, b, at + shape[2] - 1, :cols] = np.outer(sz[row], sy[yrow[-1]]).reshape(-1)
            fine = np.floor_divide(np.arange(0, shape[0], 2) + b * shape[0], BLOCK) + 1
            for side, row in ((0, yrow[0]), (1, yrow[-1])):
                block = np.einsum("zp,q->pqz", sz[fine], sy[row]).reshape(cols, -1)
                at = (lz + 2 + side) * 128
                spread[a, b, :cols, at : at + shape[0] // 2] = block
    rows = shape[1] + 2 * PAD
    expand = np.zeros((n_gx, rows, fx))
    for a in range(n_gx):
        xs = np.arange(-1, shape[1] + 1) + a * shape[1]
        block = sx[np.floor_divide(xs, BLOCK) + 1]
        expand[a, PAD - 1 : PAD + shape[1] + 1] = block
    shrink = expand.transpose(0, 2, 1)
    lam = lambda n: 2.0 - 2.0 * np.cos(math.pi * (np.arange(n) + 1.0) / (n + 1))
    total = lam(fx)[:, None] + (lam(fz)[:, None] + lam(fy)[None, :]).reshape(1, -1)
    scale = np.zeros((fx, wide))
    scale[:, :cols] = BLOCK * BLOCK * 8.0 / ((fz + 1) * (fx + 1) * (fy + 1)) / total / BLOCK**3
    return [t.astype(np.float32) for t in (spread, gather, expand, shrink, scale)]


def kernel(
    sizes, shape, heat_hbm, mat_hbm, table_hbm, spread_hbm, gather_hbm, expand_hbm, shrink_hbm, scale_hbm,
    out, heat, mat, table, kr, kb, red, black, wd, hd, dg, vsum, corr, spread, gather, expand, shrink,
    scale, s_z, r_z, s_x, r_x, s_y, r_y, got, tab_sem, send_sem, recv_sem, gsend, grecv,
):
    n_gx, n_gy, n_gz = sizes
    nz, nx, ny = shape
    lz = nz // BLOCK
    pairs = nz // 2
    rows = nx + 2 * PAD
    gx, gy, gz = lax.axis_index("gx"), lax.axis_index("gy"), lax.axis_index("gz")
    count = n_gx * n_gy * n_gz
    me = (gx * n_gy + gy) * n_gz + gz

    def peer_of(step):
        other = lax.rem(me + step, count)
        return other, {
            "gx": other // (n_gy * n_gz),
            "gy": lax.rem(other // n_gz, n_gy),
            "gz": lax.rem(other, n_gz),
        }

    inputs = [
        pltpu.make_async_copy(table_hbm, table, tab_sem.at[5]),
        pltpu.make_async_copy(mat_hbm, mat, tab_sem.at[6]),
        pltpu.make_async_copy(heat_hbm, heat, tab_sem.at[7]),
    ]
    for copy in inputs:
        copy.start()
    barrier = pltpu.get_barrier_semaphore()

    def greet(step, carry):
        _, where = peer_of(step)
        pl.semaphore_signal(barrier, inc=1, device_id=where, device_id_type=MESH)
        return carry

    lax.fori_loop(1, count, greet, 0)

    fetch = [
        pltpu.make_async_copy(spread_hbm.at[gy, gz], spread, tab_sem.at[0]),
        pltpu.make_async_copy(gather_hbm.at[gy, gz], gather, tab_sem.at[1]),
        pltpu.make_async_copy(expand_hbm.at[gx], expand, tab_sem.at[2]),
        pltpu.make_async_copy(shrink_hbm.at[gx], shrink, tab_sem.at[3]),
        pltpu.make_async_copy(scale_hbm, scale, tab_sem.at[4]),
    ]
    for copy in fetch:
        copy.start()

    faces = []
    for bufs, name, index, size, sem in (
        ((s_z, r_z), "gz", gz, n_gz, 0),
        ((s_x, r_x), "gx", gx, n_gx, 2),
    ):
        if size > 1:
            faces.append((*bufs, 0, 1, index > 0, {name: index - 1}, sem))
            faces.append((*bufs, 1, 0, index < size - 1, {name: index + 1}, sem + 1))
    single = n_gy == 2
    if single:
        edge = (ny - 1) * (1 - gy)
        edges = [edge]
        faces.append((s_y, r_y, 0, 0, None, {"gy": 1 - gy}, 4))
    else:
        edges = [0, ny - 1]
        if n_gy > 1:
            faces.append((s_y, r_y, 0, 1, gy > 0, {"gy": gy - 1}, 4))
            faces.append((s_y, r_y, 1, 0, gy < n_gy - 1, {"gy": gy + 1}, 5))

    def copies(turn, landing):
        for src, dst, mine, theirs, exists, where, sem in faces:
            there = sem if single and sem == 4 else (sem // 2) * 2 + theirs
            yield exists, pltpu.make_async_remote_copy(
                src_ref=src.at[turn, mine],
                dst_ref=dst.at[turn, mine if landing else theirs],
                send_sem=send_sem.at[turn, sem],
                recv_sem=recv_sem.at[turn, sem if landing else there],
                device_id=where,
                device_id_type=MESH,
            )

    def guarded(exists, action):
        if exists is None:
            action()
        else:
            pl.when(exists)(action)

    lane = lax.broadcasted_iota(jnp.int32, (nx, ny), 1)
    row = lax.broadcasted_iota(jnp.int32, (nx, ny), 0)
    even = lax.rem(lane + row, 2) == 0
    zero = jnp.zeros((nx, ny), jnp.float32)
    for buf, size, index in ((r_z, n_gz, gz), (r_x, n_gx, gx), (r_y, n_gy, gy)):
        if buf is r_y and single:
            continue
        for side, at in ((0, 0), (1, size - 1)):
            def clear(buf=buf, side=side):
                for turn in range(ROUNDS):
                    buf[turn, side] = jnp.zeros(buf.shape[2:], jnp.float32)

            pl.when(index == at)(clear)

    def slab(z):
        return pl.ds(pl.multiple_of(z * rows, 8) + PAD, nx)

    def packed(packs, value, z):
        result = []
        for pack, at in zip(packs, edges):
            turned = pltpu.roll(value, lax.rem(z - at + ny, ny), 1)
            result.append(jnp.where(lane == z, turned, pack))
        return tuple(result)

    blank = tuple(zero for _ in edges)

    def send(turn, field, packs):
        s_z[turn, 0] = field[pl.ds(rows + PAD, nx), :]
        s_z[turn, 1] = field[pl.ds(pairs * rows + PAD, nx), :]
        for side, at in ((0, PAD), (1, PAD + nx - 1)):
            s_x[turn, side] = field[pl.ds(rows + at, pairs, stride=rows), :]
        for side, pack in enumerate(packs):
            s_y[turn, side] = pack
        for exists, copy in copies(turn, False):
            guarded(exists, copy.start)

    def receive(turn, field):
        for exists, copy in copies(turn, True):
            guarded(exists, copy.wait_recv)
        field[pl.ds(PAD, nx), :] = r_z[turn, 0]
        field[pl.ds((pairs + 1) * rows + PAD, nx), :] = r_z[turn, 1]
        for side, at in ((0, PAD - 1), (1, PAD + nx)):
            field[pl.ds(rows + at, pairs, stride=rows), :] = r_x[turn, side]

    def beside(value, halos, z, strict):
        low, high = pltpu.roll(value, 1, 1), pltpu.roll(value, ny - 1, 1)
        if single:
            halo = pltpu.roll(halos[0], lax.rem(edge - z + ny, ny), 1)
            if strict:
                outer = gy.astype(jnp.float32)
                return (
                    jnp.where(lane == 0, halo * outer, low),
                    jnp.where(lane == ny - 1, halo * (1.0 - outer), high),
                )
            return jnp.where(lane == 0, halo, low), jnp.where(lane == ny - 1, halo, high)
        if n_gy == 1:
            return jnp.where(lane == 0, 0.0, low), jnp.where(lane == ny - 1, 0.0, high)
        first = pltpu.roll(halos[0], lax.rem(ny - z, ny), 1)
        last = pltpu.roll(halos[1], lax.rem(2 * ny - 1 - z, ny), 1)
        return jnp.where(lane == 0, first, low), jnp.where(lane == ny - 1, last, high)

    def around(field, color, halos, z, strict=False):
        same = field[slab(z + 1), :]
        before, after = field[slab(z), :], field[slab(z + 2), :]
        low, high = beside(same, halos, z, strict)
        at = pl.multiple_of((z + 1) * rows, 8) + PAD
        return (
            same,
            jnp.where(even, before, after) if color == 0 else jnp.where(even, after, before),
            field[pl.ds(at - 1, nx), :],
            field[pl.ds(at + 1, nx), :],
            low,
            high,
        )

    def y_halos(turn):
        return [r_y[turn, side] for side in range(len(edges))]

    def loop(count, step, carry, start=0):
        return lax.fori_loop(start, count, step, carry, unroll=UNROLL)

    def conduct(z, packs):
        values = []
        for layer in range(2):
            ids = mat[2 * z + layer]
            value = jnp.full((nx, ny), table[0], jnp.float32)
            for m in range(1, table.shape[0]):
                value = jnp.where(ids == m, table[m], value)
            values.append(value)
        first = jnp.where(even, values[0], values[1])
        second = jnp.where(even, values[1], values[0])
        kr[slab(z + 1), :] = first
        kb[slab(z + 1), :] = second
        return packed(packs[0], first, z), packed(packs[1], second, z)

    inputs[0].wait()
    inputs[1].wait()
    packs = loop(pairs, conduct, (blank, blank))
    pl.semaphore_wait(barrier, count - 1)
    send(0, kr, packs[0])
    send(1, kb, packs[1])
    inputs[2].wait()
    receive(0, kr)
    receive(1, kb)

    def weigh(color, own, field, turn, first):
        halos = y_halos(turn)

        def step(z, packs):
            center = own[slab(z + 1), :]
            others = around(field, color, halos, z, True)
            diag = None
            inner = []
            for other in others:
                inside = other > 0.0
                weight = 2.0 * center * other / (center + other)
                full = jnp.where(inside, weight, center)
                inner.append(jnp.where(inside, weight, 0.0))
                diag = full if diag is None else diag + full
            inverse = 1.0 / diag
            for face in range(6):
                wd[color, face, z] = inner[face] * inverse
            lower, upper = heat[2 * z], heat[2 * z + 1]
            source = jnp.where(even, lower, upper) if color == 0 else jnp.where(even, upper, lower)
            ratio = source * inverse
            hd[color, z] = ratio
            dg[color, z] = diag
            if not first:
                return packs
            red[slab(z + 1), :] = ratio
            return packed(packs, ratio, z)

        return loop(pairs, step, blank if first else 0)

    packs = weigh(0, kr, kb, 1, True)
    send(2, red, packs)
    weigh(1, kb, kr, 0, False)

    def total(color, field, halos, z):
        others = around(field, color, halos, z)
        result = hd[color, z]
        for face in range(6):
            result = result + wd[color, face, z] * others[face]
        return result

    def half(color, halos):
        field, own = ((black, red), (red, black))[color]

        def step(z, packs):
            value = total(color, field, halos, z)
            own[slab(z + 1), :] = value
            return packed(packs, value, z)

        return loop(pairs, step, blank)

    for turn, color in ((3, 1), (4, 0), (5, 1)):
        receive(turn - 1, (black, red)[color])
        packs = half(color, y_halos(turn - 1))
        send(turn, (red, black)[color], packs)

    black[pl.ds(PAD, nx), :] = zero
    black[pl.ds((pairs + 1) * rows + PAD, nx), :] = zero
    for at in (PAD - 1, PAD + nx):
        black[pl.ds(rows + at, pairs, stride=rows), :] = jnp.zeros((pairs, ny), jnp.float32)
    vsum[...] = jnp.zeros(vsum.shape, jnp.float32)
    tile = jnp.zeros((8, ny), jnp.float32)
    tile_row = lax.broadcasted_iota(jnp.int32, (8, ny), 0)

    def outward(z):
        return dg[1, z] * black[slab(z + 1), :]

    for layer in range(lz):
        def gap(z, sums):
            inner, low, high, ends = sums
            flow = outward(z)
            inner = inner + dg[0, z] * (total(0, black, blank, z) - red[slab(z + 1), :])
            low = low + (wd[1, 2, z] * flow)[:8]
            high = high + (wd[1, 3, z] * flow)[nx - 8 :]
            weight = jnp.where(lane == 0, wd[1, 4, z], jnp.where(lane == ny - 1, wd[1, 5, z], 0.0))
            return inner, low, high, ends + weight * flow

        inner, low, high, ends = loop(
            (layer + 1) * BLOCK // 2, gap, (zero, tile, tile, zero), layer * BLOCK // 2
        )
        here = slice((layer + 1) * ny, (layer + 2) * ny)
        vsum[PAD : PAD + nx, here] = inner
        vsum[PAD - 8 : PAD, here] = jnp.where(tile_row == 7, pltpu.roll(low, 7, 0), 0.0)
        vsum[PAD + nx : PAD + nx + 8, here] = jnp.where(tile_row == 0, pltpu.roll(high, 1, 0), 0.0)
        vsum[PAD : PAD + nx, (lz + 2 + layer) * ny : (lz + 3 + layer) * ny] = ends
    vsum[PAD : PAD + nx, :ny] = jnp.where(even, 0.0, wd[1, 1, 0] * outward(0))
    vsum[PAD : PAD + nx, (lz + 1) * ny : (lz + 2) * ny] = jnp.where(
        even, wd[1, 1, pairs - 1] * outward(pairs - 1), 0.0
    )
    for copy in fetch:
        copy.wait()
    part = jnp.dot(shrink[...], vsum[...], precision=HIGH, preferred_element_type=jnp.float32)
    part = jnp.dot(part, gather[...], precision=HIGH, preferred_element_type=jnp.float32)
    got[me] = part

    def gathering(step, start):
        other, where = peer_of(step)
        copy = pltpu.make_async_remote_copy(
            src_ref=got.at[me],
            dst_ref=got.at[me if start else other],
            send_sem=gsend.at[step],
            recv_sem=grecv.at[me if start else other],
            device_id=where,
            device_id_type=MESH,
        )
        return copy

    def give(step, carry):
        gathering(step, True).start()
        return carry

    def take(step, carry):
        gathering(step, False).wait_recv()
        return carry

    lax.fori_loop(1, count, give, 0)
    receive(5, black)
    halos = y_halos(5)
    lax.fori_loop(1, count, take, 0)
    if count <= 32:
        hat = got[0]
        for i in range(1, count):
            hat = hat + got[i]
    else:
        hat = lax.fori_loop(1, count, lambda i, acc: acc + got[i], got[0])
    kbar = table[0]
    for m in range(1, table.shape[0]):
        kbar = kbar + table[m]
    kbar = kbar / table.shape[0]
    hat = hat * scale[...] / kbar
    hat = jnp.dot(hat, spread[...], precision=HIGH, preferred_element_type=jnp.float32)
    corr[...] = jnp.dot(expand[...], hat, precision=HIGH, preferred_element_type=jnp.float32)

    def correct(z, carry):
        layer = (z + BLOCK // 2 - 1) // (BLOCK // 2)
        at = pl.ds(pl.multiple_of(z * rows, 8), rows)
        black[at, :] = black[at, :] + corr[:, pl.ds(pl.multiple_of(layer * ny, ny), ny)]
        return carry

    lax.fori_loop(0, pairs + 2, correct, 0, unroll=2)
    sides = [corr[PAD : PAD + nx, (lz + 2 + s) * ny : (lz + 3 + s) * ny] for s in range(2)]
    if single:
        upper = gy.astype(jnp.float32)
        halos = [halos[0] + sides[0] * upper + sides[1] * (1.0 - upper)]
    else:
        halos = [halo + side for halo, side in zip(halos, sides)]

    packs = half(0, halos)
    send(6, red, packs)
    for turn, color in ((7, 1), (8, 0)):
        receive(turn - 1, (black, red)[color])
        packs = half(color, y_halos(turn - 1))
        send(turn, (red, black)[color], packs)
    receive(8, red)
    halos = y_halos(8)

    def finish(z, carry):
        last = total(1, red, halos, z)
        own = red[slab(z + 1), :]
        out[2 * z] = jnp.where(even, own, last)
        out[2 * z + 1] = jnp.where(even, last, own)
        return carry

    loop(pairs, finish, 0)

    for turn in range(ROUNDS):
        for exists, copy in copies(turn, False):
            guarded(exists, copy.wait_send)

    def sent(step, carry):
        gathering(step, True).wait_send()
        return carry

    lax.fori_loop(1, count, sent, 0)


def per_device(sizes, heat, material, table):
    shape = heat.shape
    nz, nx, ny = shape
    n_gx, n_gy, n_gz = sizes
    consts = tables(shape, *sizes)
    spread, gather, expand, shrink, scale = consts
    count = n_gx * n_gy * n_gz
    rows = nx + 2 * PAD
    sides = 1 if n_gy == 2 else 2
    f32 = jnp.float32
    vmem = pl.BlockSpec(memory_space=pltpu.VMEM)
    hbm = pl.BlockSpec(memory_space=pltpu.HBM)
    faces = [
        pltpu.VMEM((ROUNDS, 2, nx, ny), f32),
        pltpu.VMEM((ROUNDS, 2, nx, ny), f32),
        pltpu.VMEM((ROUNDS, 2, nz // 2, ny), f32),
        pltpu.VMEM((ROUNDS, 2, nz // 2, ny), f32),
        pltpu.VMEM((ROUNDS, sides, nx, ny), f32),
        pltpu.VMEM((ROUNDS, sides, nx, ny), f32),
    ]
    return pl.pallas_call(
        functools.partial(kernel, sizes, shape),
        out_shape=jax.ShapeDtypeStruct(shape, f32),
        in_specs=[hbm] * 8,
        out_specs=vmem,
        scratch_shapes=[
            pltpu.VMEM(shape, f32),
            pltpu.VMEM(shape, jnp.int32),
            pltpu.SMEM(table.shape, f32),
            *[pltpu.VMEM(((nz // 2 + 2) * rows, ny), f32)] * 4,
            pltpu.VMEM((2, 6, nz // 2, nx, ny), f32),
            pltpu.VMEM((2, nz // 2, nx, ny), f32),
            pltpu.VMEM((2, nz // 2, nx, ny), f32),
            pltpu.VMEM((rows, gather.shape[2]), f32),
            pltpu.VMEM((rows, spread.shape[3]), f32),
            pltpu.VMEM(spread.shape[2:], f32),
            pltpu.VMEM(gather.shape[2:], f32),
            pltpu.VMEM(expand.shape[1:], f32),
            pltpu.VMEM(shrink.shape[1:], f32),
            pltpu.VMEM(scale.shape, f32),
            *faces,
            pltpu.VMEM((count, *scale.shape), f32),
            pltpu.SemaphoreType.DMA((8,)),
            pltpu.SemaphoreType.DMA((ROUNDS, 6)),
            pltpu.SemaphoreType.DMA((ROUNDS, 6)),
            pltpu.SemaphoreType.DMA((count,)),
            pltpu.SemaphoreType.DMA((count,)),
        ],
        compiler_params=pltpu.CompilerParams(
            collective_id=0, has_side_effects=True, vmem_limit_bytes=64 * 1024 * 1024
        ),
    )(heat, material, table, *(jnp.asarray(c) for c in consts))


def solution(mesh):
    sizes = (mesh.shape["gx"], mesh.shape["gy"], mesh.shape["gz"])
    spec = P("gz", ("groups", "gx"), "gy")
    return jax.shard_map(
        functools.partial(per_device, sizes),
        mesh=mesh,
        in_specs=(spec, spec, P()),
        out_specs=spec,
        check_vma=False,
    )
```

```python
import functools
import math

import jax
import jax.numpy as jnp
import numpy as np
from jax import lax
from jax.experimental import pallas as pl
from jax.experimental.pallas import tpu as pltpu
from jax.sharding import PartitionSpec as P

BLOCK = 16
PAD = 8
UNROLL = 8
MESH = pl.DeviceIdType.MESH
HIGH = lax.Precision.HIGHEST
ROUNDS = 9


def sine_rows(count):
    j = np.arange(-1, count + 1)[:, None] + 1.0
    k = np.arange(count)[None, :] + 1.0
    rows = np.sin(math.pi * j * k / (count + 1))
    rows[0] = 0.0
    rows[-1] = 0.0
    return rows


def tables(shape, n_gx, n_gy, n_gz):
    lz, lx, ly = (s // BLOCK for s in shape)
    fz, fx, fy = lz * n_gz, lx * n_gx, ly * n_gy
    cols = fz * fy
    wide = -(-cols // 128) * 128
    sz, sx, sy = sine_rows(fz), sine_rows(fx), sine_rows(fy)
    zs = np.arange(-1, shape[0] + 1)
    ys = np.arange(-1, shape[2] + 1)
    spread = np.zeros((n_gy, n_gz, wide, (lz + 4) * 128))
    gather = np.zeros((n_gy, n_gz, (2 * lz + 2) * 128, wide))
    for a in range(n_gy):
        yrow = np.floor_divide(ys + a * shape[2], BLOCK) + 1
        for b in range(n_gz):
            zrow = np.arange(-1, lz + 1) + b * lz + 1
            for i, row in enumerate(zrow):
                block = np.einsum("p,yq->pqy", sz[row], sy[yrow[1:-1]]).reshape(cols, -1)
                spread[a, b, :cols, i * 128 : i * 128 + shape[2]] = block
                gather[a, b, i * 128 : i * 128 + shape[2], :cols] = block.T
                if 1 <= i <= lz:
                    at = (lz + 1 + i) * 128
                    gather[a, b, at, :cols] = np.outer(sz[row], sy[yrow[0]]).reshape(-1)
                    gather[a, b, at + shape[2] - 1, :cols] = np.outer(sz[row], sy[yrow[-1]]).reshape(-1)
            fine = np.floor_divide(np.arange(0, shape[0], 2) + b * shape[0], BLOCK) + 1
            for side, row in ((0, yrow[0]), (1, yrow[-1])):
                block = np.einsum("zp,q->pqz", sz[fine], sy[row]).reshape(cols, -1)
                at = (lz + 2 + side) * 128
                spread[a, b, :cols, at : at + shape[0] // 2] = block
    rows = shape[1] + 2 * PAD
    expand = np.zeros((n_gx, rows, fx))
    for a in range(n_gx):
        xs = np.arange(-1, shape[1] + 1) + a * shape[1]
        block = sx[np.floor_divide(xs, BLOCK) + 1]
        expand[a, PAD - 1 : PAD + shape[1] + 1] = block
    shrink = expand.transpose(0, 2, 1)
    lam = lambda n: 2.0 - 2.0 * np.cos(math.pi * (np.arange(n) + 1.0) / (n + 1))
    total = lam(fx)[:, None] + (lam(fz)[:, None] + lam(fy)[None, :]).reshape(1, -1)
    scale = np.zeros((fx, wide))
    scale[:, :cols] = BLOCK * BLOCK * 8.0 / ((fz + 1) * (fx + 1) * (fy + 1)) / total / BLOCK**3
    return [t.astype(np.float32) for t in (spread, gather, expand, shrink, scale)]


def kernel(
    sizes, shape, heat_hbm, mat_hbm, table_hbm, spread_hbm, gather_hbm, expand_hbm, shrink_hbm, scale_hbm,
    out, heat, mat, table, kr, kb, red, black, ahead, wd, wxf, wyf, hd, dg, vsum, corr, spread, gather, expand, shrink,
    scale, s_z, r_z, s_x, r_x, s_y, r_y, got, tab_sem, send_sem, recv_sem, gsend, grecv,
):
    n_gx, n_gy, n_gz = sizes
    nz, nx, ny = shape
    lz = nz // BLOCK
    pairs = nz // 2
    rows = nx + 2 * PAD
    gx, gy, gz = lax.axis_index("gx"), lax.axis_index("gy"), lax.axis_index("gz")
    count = n_gx * n_gy * n_gz
    me = (gx * n_gy + gy) * n_gz + gz

    few = count <= 32
    offsets = sorted(
        ((a, b, c) for a in range(n_gx) for b in range(n_gy) for c in range(n_gz) if a or b or c),
        key=lambda o: (-min(o[0], n_gx - o[0]), -min(o[1], n_gy - o[1]), -o[2]),
    )

    def turned(position, step, size):
        at = position + step
        return jnp.where(at >= size, at - size, at)

    def peer_of(step):
        if few:
            a, b, c = offsets[step - 1]
            at = turned(gx, a, n_gx), turned(gy, b, n_gy), turned(gz, c, n_gz)
            return (at[0] * n_gy + at[1]) * n_gz + at[2], dict(zip(("gx", "gy", "gz"), at))
        other = lax.rem(me + step, count)
        return other, {
            "gx": other // (n_gy * n_gz),
            "gy": lax.rem(other // n_gz, n_gy),
            "gz": lax.rem(other, n_gz),
        }

    def each_peer(action):
        if few:
            for step in range(1, count):
                action(step)
            return

        def one(step, carry):
            action(step)
            return carry

        lax.fori_loop(1, count, one, 0)

    inputs = [
        pltpu.make_async_copy(table_hbm, table, tab_sem.at[5]),
        pltpu.make_async_copy(mat_hbm, mat, tab_sem.at[6]),
        pltpu.make_async_copy(heat_hbm, heat, tab_sem.at[7]),
    ]
    for copy in inputs:
        copy.start()
    barrier = pltpu.get_barrier_semaphore()

    def greet(step):
        _, where = peer_of(step)
        pl.semaphore_signal(barrier, inc=1, device_id=where, device_id_type=MESH)

    each_peer(greet)

    fetch = [
        pltpu.make_async_copy(spread_hbm.at[gy, gz], spread, tab_sem.at[0]),
        pltpu.make_async_copy(gather_hbm.at[gy, gz], gather, tab_sem.at[1]),
        pltpu.make_async_copy(expand_hbm.at[gx], expand, tab_sem.at[2]),
        pltpu.make_async_copy(shrink_hbm.at[gx], shrink, tab_sem.at[3]),
        pltpu.make_async_copy(scale_hbm, scale, tab_sem.at[4]),
    ]
    for copy in fetch:
        copy.start()

    faces = []
    for bufs, name, index, size, sem in (
        ((s_z, r_z), "gz", gz, n_gz, 0),
        ((s_x, r_x), "gx", gx, n_gx, 2),
    ):
        if size > 1:
            faces.append((*bufs, 0, 1, index > 0, {name: index - 1}, sem))
            faces.append((*bufs, 1, 0, index < size - 1, {name: index + 1}, sem + 1))
    single = n_gy == 2
    if single:
        edge = (ny - 1) * (1 - gy)
        edges = [edge]
        faces.append((s_y, r_y, 0, 0, None, {"gy": 1 - gy}, 4))
    else:
        edges = [0, ny - 1]
        if n_gy > 1:
            faces.append((s_y, r_y, 0, 1, gy > 0, {"gy": gy - 1}, 4))
            faces.append((s_y, r_y, 1, 0, gy < n_gy - 1, {"gy": gy + 1}, 5))

    def copies(turn, landing):
        for src, dst, mine, theirs, exists, where, sem in faces:
            there = sem if single and sem == 4 else (sem // 2) * 2 + theirs
            yield exists, pltpu.make_async_remote_copy(
                src_ref=src.at[turn, mine],
                dst_ref=dst.at[turn, mine if landing else theirs],
                send_sem=send_sem.at[turn, sem],
                recv_sem=recv_sem.at[turn, sem if landing else there],
                device_id=where,
                device_id_type=MESH,
            )

    def guarded(exists, action):
        if exists is None:
            action()
        else:
            pl.when(exists)(action)

    lane = lax.broadcasted_iota(jnp.int32, (nx, ny), 1)
    row = lax.broadcasted_iota(jnp.int32, (nx, ny), 0)
    even = lax.rem(lane + row, 2) == 0
    zero = jnp.zeros((nx, ny), jnp.float32)
    for buf, size, index in ((r_z, n_gz, gz), (r_x, n_gx, gx), (r_y, n_gy, gy)):
        if buf is r_y and single:
            continue
        for side, at in ((0, 0), (1, size - 1)):
            def clear(buf=buf, side=side):
                for turn in range(ROUNDS):
                    buf[turn, side] = jnp.zeros(buf.shape[2:], jnp.float32)

            pl.when(index == at)(clear)

    def slab(z):
        return pl.ds(pl.multiple_of(z * rows, 8) + PAD, nx)

    def packed(packs, value, z):
        result = []
        for pack, at in zip(packs, edges):
            turned = pltpu.roll(value, lax.rem(z - at + ny, ny), 1)
            result.append(jnp.where(lane == z, turned, pack))
        return tuple(result)

    blank = tuple(zero for _ in edges)

    def send(turn, field, packs):
        s_z[turn, 0] = field[pl.ds(rows + PAD, nx), :]
        s_z[turn, 1] = field[pl.ds(pairs * rows + PAD, nx), :]
        for side, at in ((0, PAD), (1, PAD + nx - 1)):
            s_x[turn, side] = field[pl.ds(rows + at, pairs, stride=rows), :]
        for side, pack in enumerate(packs):
            s_y[turn, side] = pack
        for exists, copy in copies(turn, False):
            guarded(exists, copy.start)

    def receive(turn, field):
        for exists, copy in copies(turn, True):
            guarded(exists, copy.wait_recv)
        field[pl.ds(PAD, nx), :] = r_z[turn, 0]
        field[pl.ds((pairs + 1) * rows + PAD, nx), :] = r_z[turn, 1]
        for side, at in ((0, PAD - 1), (1, PAD + nx)):
            field[pl.ds(rows + at, pairs, stride=rows), :] = r_x[turn, side]

    def beside(value, halos, z, strict):
        low, high = pltpu.roll(value, 1, 1), pltpu.roll(value, ny - 1, 1)
        if single:
            halo = pltpu.roll(halos[0], lax.rem(edge - z + ny, ny), 1)
            if strict:
                outer = gy.astype(jnp.float32)
                return (
                    jnp.where(lane == 0, halo * outer, low),
                    jnp.where(lane == ny - 1, halo * (1.0 - outer), high),
                )
            return jnp.where(lane == 0, halo, low), jnp.where(lane == ny - 1, halo, high)
        if n_gy == 1:
            return jnp.where(lane == 0, 0.0, low), jnp.where(lane == ny - 1, 0.0, high)
        first = pltpu.roll(halos[0], lax.rem(ny - z, ny), 1)
        last = pltpu.roll(halos[1], lax.rem(2 * ny - 1 - z, ny), 1)
        return jnp.where(lane == 0, first, low), jnp.where(lane == ny - 1, last, high)

    def around(field, color, halos, z, strict=False):
        same = field[slab(z + 1), :]
        before, after = field[slab(z), :], field[slab(z + 2), :]
        low, high = beside(same, halos, z, strict)
        at = pl.multiple_of((z + 1) * rows, 8) + PAD
        return (
            same,
            jnp.where(even, before, after) if color == 0 else jnp.where(even, after, before),
            field[pl.ds(at - 1, nx), :],
            field[pl.ds(at + 1, nx), :],
            low,
            high,
        )

    def y_halos(turn):
        return [r_y[turn, side] for side in range(len(edges))]

    def loop(count, step, carry, start=0):
        return lax.fori_loop(start, count, step, carry, unroll=UNROLL)

    def conduct(z, packs):
        values = []
        for layer in range(2):
            ids = mat[2 * z + layer]
            value = jnp.full((nx, ny), table[0], jnp.float32)
            for m in range(1, table.shape[0]):
                value = jnp.where(ids == m, table[m], value)
            values.append(value)
        first = jnp.where(even, values[0], values[1])
        second = jnp.where(even, values[1], values[0])
        kr[slab(z + 1), :] = first
        kb[slab(z + 1), :] = second
        return packed(packs[0], first, z), packed(packs[1], second, z)

    inputs[0].wait()
    inputs[1].wait()
    packs = loop(pairs, conduct, (blank, blank))
    pl.semaphore_wait(barrier, count - 1)
    send(0, kr, packs[0])
    send(1, kb, packs[1])
    inputs[2].wait()
    receive(0, kr)
    receive(1, kb)

    def quiet(field):
        field[pl.ds(PAD, nx), :] = zero
        field[pl.ds((pairs + 1) * rows + PAD, nx), :] = zero
        for at in (PAD - 1, PAD + nx):
            field[pl.ds(rows + at, pairs, stride=rows), :] = jnp.zeros((pairs, ny), jnp.float32)

    def weigh(color, own, field, turn, first):
        halos = y_halos(turn)

        def step(z, carry):
            packs, edge_packs = carry
            center = own[slab(z + 1), :]
            others = around(field, color, halos, z, True)
            diag = None
            inner = []
            for other in others:
                inside = other > 0.0
                weight = 2.0 * center * other / (center + other)
                full = jnp.where(inside, weight, center)
                inner.append(jnp.where(inside, weight, 0.0))
                diag = full if diag is None else diag + full
            inverse = 1.0 / diag
            for face in range(6):
                inner[face] = inner[face] * inverse
                wd[color, face, z] = inner[face]
            wxf[color, 0, pl.ds(z, 1), :] = inner[2][:1]
            wxf[color, 1, pl.ds(z, 1), :] = inner[3][nx - 1 :]
            edge_packs = packed(edge_packs, jnp.where(lane == 0, inner[4], inner[5]), z)
            lower, upper = heat[2 * z], heat[2 * z + 1]
            source = jnp.where(even, lower, upper) if color == 0 else jnp.where(even, upper, lower)
            ratio = source * inverse
            hd[color, z] = ratio
            dg[color, z] = diag
            if not first:
                return packs, edge_packs
            red[slab(z + 1), :] = ratio
            return packed(packs, ratio, z), edge_packs

        packs, edge_packs = loop(pairs, step, (blank, blank))
        for side, pack in enumerate(edge_packs):
            wyf[color, side] = pack
        return packs

    quiet(red)
    packs = weigh(0, kr, kb, 1, True)
    send(2, red, packs)
    weigh(1, kb, kr, 0, False)

    def total(color, field, halos, z):
        others = around(field, color, halos, z)
        result = hd[color, z]
        for face in range(6):
            result = result + wd[color, face, z] * others[face]
        return result

    def early(color, halos=blank):
        field = (black, red)[color]

        def step(z, carry):
            ahead[slab(z + 1), :] = total(color, field, halos, z)
            return carry

        loop(pairs, step, 0)

    def late(turn, color, store, carry):
        for exists, copy in copies(turn, True):
            guarded(exists, copy.wait_recv)
        for side, z in ((0, 0), (1, pairs - 1)):
            term = wd[color, 1, z] * r_z[turn, side]
            mine = even if side == color else jnp.logical_not(even)
            ahead[slab(z + 1), :] = ahead[slab(z + 1), :] + jnp.where(mine, term, 0.0)
        for side, at in ((0, PAD), (1, PAD + nx - 1)):
            where = pl.ds(rows + at, pairs, stride=rows)
            ahead[where, :] = ahead[where, :] + wxf[color, side] * r_x[turn, side]
        terms = [wyf[color, side] * r_y[turn, side] for side in range(len(edges))]

        def step(z, carry):
            value = ahead[slab(z + 1), :]
            for term, at in zip(terms, edges):
                term = pltpu.roll(term, lax.rem(at - z + ny, ny), 1)
                value = jnp.where(lane == at, value + term, value)
            return store(z, value, carry)

        return loop(pairs, step, carry)

    def finished(turn, color):
        own = (red, black)[color]

        def store(z, value, packs):
            own[slab(z + 1), :] = value
            return packed(packs, value, z)

        return late(turn, color, store, blank)

    quiet(black)
    for turn, color in ((3, 1), (4, 0), (5, 1)):
        early(color)
        packs = finished(turn - 1, color)
        send(turn, (red, black)[color], packs)

    vsum[...] = jnp.zeros(vsum.shape, jnp.float32)
    tile = jnp.zeros((8, ny), jnp.float32)
    tile_row = lax.broadcasted_iota(jnp.int32, (8, ny), 0)

    def outward(z):
        return dg[1, z] * black[slab(z + 1), :]

    for layer in range(lz):
        def gap(z, sums):
            inner, low, high, ends = sums
            flow = outward(z)
            inner = inner + dg[0, z] * (total(0, black, blank, z) - red[slab(z + 1), :])
            low = low + (wd[1, 2, z] * flow)[:8]
            high = high + (wd[1, 3, z] * flow)[nx - 8 :]
            weight = jnp.where(lane == 0, wd[1, 4, z], jnp.where(lane == ny - 1, wd[1, 5, z], 0.0))
            return inner, low, high, ends + weight * flow

        inner, low, high, ends = loop(
            (layer + 1) * BLOCK // 2, gap, (zero, tile, tile, zero), layer * BLOCK // 2
        )
        here = slice((layer + 1) * ny, (layer + 2) * ny)
        vsum[PAD : PAD + nx, here] = inner
        vsum[PAD - 8 : PAD, here] = jnp.where(tile_row == 7, pltpu.roll(low, 7, 0), 0.0)
        vsum[PAD + nx : PAD + nx + 8, here] = jnp.where(tile_row == 0, pltpu.roll(high, 1, 0), 0.0)
        vsum[PAD : PAD + nx, (lz + 2 + layer) * ny : (lz + 3 + layer) * ny] = ends
    vsum[PAD : PAD + nx, :ny] = jnp.where(even, 0.0, wd[1, 1, 0] * outward(0))
    vsum[PAD : PAD + nx, (lz + 1) * ny : (lz + 2) * ny] = jnp.where(
        even, wd[1, 1, pairs - 1] * outward(pairs - 1), 0.0
    )
    for copy in fetch:
        copy.wait()
    part = jnp.dot(shrink[...], vsum[...], precision=HIGH, preferred_element_type=jnp.float32)
    part = jnp.dot(part, gather[...], precision=HIGH, preferred_element_type=jnp.float32)
    got[me] = part

    def gathering(step, start):
        other, where = peer_of(step)
        copy = pltpu.make_async_remote_copy(
            src_ref=got.at[me],
            dst_ref=got.at[me if start else other],
            send_sem=gsend.at[step],
            recv_sem=grecv.at[me if start else other],
            device_id=where,
            device_id_type=MESH,
        )
        return copy

    each_peer(lambda step: gathering(step, True).start())
    each_peer(lambda step: gathering(step, False).wait_recv())
    if count <= 32:
        hat = got[0]
        for i in range(1, count):
            hat = hat + got[i]
    else:
        hat = lax.fori_loop(1, count, lambda i, acc: acc + got[i], got[0])
    kbar = table[0]
    for m in range(1, table.shape[0]):
        kbar = kbar + table[m]
    kbar = kbar / table.shape[0]
    hat = hat * scale[...] / kbar
    hat = jnp.dot(hat, spread[...], precision=HIGH, preferred_element_type=jnp.float32)
    corr[...] = jnp.dot(expand[...], hat, precision=HIGH, preferred_element_type=jnp.float32)

    def correct(z, carry):
        layer = (z + BLOCK // 2 - 1) // (BLOCK // 2)
        at = pl.ds(pl.multiple_of(z * rows, 8), rows)
        black[at, :] = black[at, :] + corr[:, pl.ds(pl.multiple_of(layer * ny, ny), ny)]
        return carry

    lax.fori_loop(0, pairs + 2, correct, 0, unroll=2)
    sides = [corr[PAD : PAD + nx, (lz + 2 + s) * ny : (lz + 3 + s) * ny] for s in range(2)]
    if single:
        upper = gy.astype(jnp.float32)
        sides = [sides[0] * upper + sides[1] * (1.0 - upper)]
    early(0, sides)
    quiet(black)
    packs = finished(5, 0)
    send(6, red, packs)
    for turn, color in ((7, 1), (8, 0)):
        early(color)
        packs = finished(turn - 1, color)
        send(turn, (red, black)[color], packs)
    early(1)

    def finish(z, last, carry):
        own = red[slab(z + 1), :]
        out[2 * z] = jnp.where(even, own, last)
        out[2 * z + 1] = jnp.where(even, last, own)
        return carry

    late(8, 1, finish, 0)

    for turn in range(ROUNDS):
        for exists, copy in copies(turn, False):
            guarded(exists, copy.wait_send)

    each_peer(lambda step: gathering(step, True).wait_send())


def per_device(sizes, heat, material, table):
    shape = heat.shape
    nz, nx, ny = shape
    n_gx, n_gy, n_gz = sizes
    consts = tables(shape, *sizes)
    spread, gather, expand, shrink, scale = consts
    count = n_gx * n_gy * n_gz
    rows = nx + 2 * PAD
    sides = 1 if n_gy == 2 else 2
    f32 = jnp.float32
    vmem = pl.BlockSpec(memory_space=pltpu.VMEM)
    hbm = pl.BlockSpec(memory_space=pltpu.HBM)
    faces = [
        pltpu.VMEM((ROUNDS, 2, nx, ny), f32),
        pltpu.VMEM((ROUNDS, 2, nx, ny), f32),
        pltpu.VMEM((ROUNDS, 2, nz // 2, ny), f32),
        pltpu.VMEM((ROUNDS, 2, nz // 2, ny), f32),
        pltpu.VMEM((ROUNDS, sides, nx, ny), f32),
        pltpu.VMEM((ROUNDS, sides, nx, ny), f32),
    ]
    return pl.pallas_call(
        functools.partial(kernel, sizes, shape),
        out_shape=jax.ShapeDtypeStruct(shape, f32),
        in_specs=[hbm] * 8,
        out_specs=vmem,
        scratch_shapes=[
            pltpu.VMEM(shape, f32),
            pltpu.VMEM(shape, jnp.int32),
            pltpu.SMEM(table.shape, f32),
            *[pltpu.VMEM(((nz // 2 + 2) * rows, ny), f32)] * 5,
            pltpu.VMEM((2, 6, nz // 2, nx, ny), f32),
            pltpu.VMEM((2, 2, nz // 2, ny), f32),
            pltpu.VMEM((2, sides, nx, ny), f32),
            pltpu.VMEM((2, nz // 2, nx, ny), f32),
            pltpu.VMEM((2, nz // 2, nx, ny), f32),
            pltpu.VMEM((rows, gather.shape[2]), f32),
            pltpu.VMEM((rows, spread.shape[3]), f32),
            pltpu.VMEM(spread.shape[2:], f32),
            pltpu.VMEM(gather.shape[2:], f32),
            pltpu.VMEM(expand.shape[1:], f32),
            pltpu.VMEM(shrink.shape[1:], f32),
            pltpu.VMEM(scale.shape, f32),
            *faces,
            pltpu.VMEM((count, *scale.shape), f32),
            pltpu.SemaphoreType.DMA((8,)),
            pltpu.SemaphoreType.DMA((ROUNDS, 6)),
            pltpu.SemaphoreType.DMA((ROUNDS, 6)),
            pltpu.SemaphoreType.DMA((count,)),
            pltpu.SemaphoreType.DMA((count,)),
        ],
        compiler_params=pltpu.CompilerParams(
            collective_id=0, has_side_effects=True, vmem_limit_bytes=64 * 1024 * 1024
        ),
    )(heat, material, table, *(jnp.asarray(c) for c in consts))


def solution(mesh):
    sizes = (mesh.shape["gx"], mesh.shape["gy"], mesh.shape["gz"])
    spec = P("gz", ("groups", "gx"), "gy")
    return jax.shard_map(
        functools.partial(per_device, sizes),
        mesh=mesh,
        in_specs=(spec, spec, P()),
        out_specs=spec,
        check_vma=False,
    )
```

```python
import functools
import math

import jax
import jax.numpy as jnp
import numpy as np
from jax import lax
from jax.experimental import pallas as pl
from jax.experimental.pallas import tpu as pltpu
from jax.sharding import PartitionSpec as P

BLOCK = 16
PAD = 8
UNROLL = 8
MESH = pl.DeviceIdType.MESH
HIGH = lax.Precision.HIGHEST
ROUNDS = 9


def sine_rows(count):
    j = np.arange(-1, count + 1)[:, None] + 1.0
    k = np.arange(count)[None, :] + 1.0
    rows = np.sin(math.pi * j * k / (count + 1))
    rows[0] = 0.0
    rows[-1] = 0.0
    return rows


def tables(shape, n_gx, n_gy, n_gz):
    lz, lx, ly = (s // BLOCK for s in shape)
    fz, fx, fy = lz * n_gz, lx * n_gx, ly * n_gy
    cols = fz * fy
    wide = -(-cols // 128) * 128
    sz, sx, sy = sine_rows(fz), sine_rows(fx), sine_rows(fy)
    zs = np.arange(-1, shape[0] + 1)
    ys = np.arange(-1, shape[2] + 1)
    spread = np.zeros((n_gy, n_gz, wide, (lz + 4) * 128))
    gather = np.zeros((n_gy, n_gz, (2 * lz + 2) * 128, wide))
    for a in range(n_gy):
        yrow = np.floor_divide(ys + a * shape[2], BLOCK) + 1
        for b in range(n_gz):
            zrow = np.arange(-1, lz + 1) + b * lz + 1
            for i, row in enumerate(zrow):
                block = np.einsum("p,yq->pqy", sz[row], sy[yrow[1:-1]]).reshape(cols, -1)
                spread[a, b, :cols, i * 128 : i * 128 + shape[2]] = block
                gather[a, b, i * 128 : i * 128 + shape[2], :cols] = block.T
                if 1 <= i <= lz:
                    at = (lz + 1 + i) * 128
                    gather[a, b, at, :cols] = np.outer(sz[row], sy[yrow[0]]).reshape(-1)
                    gather[a, b, at + shape[2] - 1, :cols] = np.outer(sz[row], sy[yrow[-1]]).reshape(-1)
            fine = np.floor_divide(np.arange(0, shape[0], 2) + b * shape[0], BLOCK) + 1
            for side, row in ((0, yrow[0]), (1, yrow[-1])):
                block = np.einsum("zp,q->pqz", sz[fine], sy[row]).reshape(cols, -1)
                at = (lz + 2 + side) * 128
                spread[a, b, :cols, at : at + shape[0] // 2] = block
    rows = shape[1] + 2 * PAD
    expand = np.zeros((n_gx, rows, fx))
    for a in range(n_gx):
        xs = np.arange(-1, shape[1] + 1) + a * shape[1]
        block = sx[np.floor_divide(xs, BLOCK) + 1]
        expand[a, PAD - 1 : PAD + shape[1] + 1] = block
    shrink = expand.transpose(0, 2, 1)
    lam = lambda n: 2.0 - 2.0 * np.cos(math.pi * (np.arange(n) + 1.0) / (n + 1))
    total = lam(fx)[:, None] + (lam(fz)[:, None] + lam(fy)[None, :]).reshape(1, -1)
    scale = np.zeros((fx, wide))
    scale[:, :cols] = BLOCK * BLOCK * 8.0 / ((fz + 1) * (fx + 1) * (fy + 1)) / total / BLOCK**3
    return [t.astype(np.float32) for t in (spread, gather, expand, shrink, scale)]


def kernel(
    sizes, shape, heat_hbm, mat_hbm, table_hbm, spread_hbm, gather_hbm, expand_hbm, shrink_hbm, scale_hbm,
    out, heat, mat, table, kr, kb, red, black, ahead, wd, wxf, wyf, hd, dg, vsum, corr, spread, gather, expand, shrink,
    scale, s_z, r_z, s_x, r_x, s_y, r_y, got, tab_sem, send_sem, recv_sem, gsend, grecv,
):
    n_gx, n_gy, n_gz = sizes
    nz, nx, ny = shape
    lz = nz // BLOCK
    pairs = nz // 2
    rows = nx + 2 * PAD
    gx, gy, gz = lax.axis_index("gx"), lax.axis_index("gy"), lax.axis_index("gz")
    count = n_gx * n_gy * n_gz
    me = (gx * n_gy + gy) * n_gz + gz

    few = count <= 32
    offsets = sorted(
        ((a, b, c) for a in range(n_gx) for b in range(n_gy) for c in range(n_gz) if a or b or c),
        key=lambda o: (-min(o[0], n_gx - o[0]), -min(o[1], n_gy - o[1]), -o[2]),
    )

    def turned(position, step, size):
        at = position + step
        return jnp.where(at >= size, at - size, at)

    def peer_of(step):
        if few:
            a, b, c = offsets[step - 1]
            at = turned(gx, a, n_gx), turned(gy, b, n_gy), turned(gz, c, n_gz)
            return (at[0] * n_gy + at[1]) * n_gz + at[2], dict(zip(("gx", "gy", "gz"), at))
        other = lax.rem(me + step, count)
        return other, {
            "gx": other // (n_gy * n_gz),
            "gy": lax.rem(other // n_gz, n_gy),
            "gz": lax.rem(other, n_gz),
        }

    def each_peer(action):
        if few:
            for step in range(1, count):
                action(step)
            return

        def one(step, carry):
            action(step)
            return carry

        lax.fori_loop(1, count, one, 0)

    inputs = [
        pltpu.make_async_copy(table_hbm, table, tab_sem.at[5]),
        pltpu.make_async_copy(mat_hbm, mat, tab_sem.at[6]),
        pltpu.make_async_copy(heat_hbm, heat, tab_sem.at[7]),
    ]
    for copy in inputs:
        copy.start()
    barrier = pltpu.get_barrier_semaphore()

    def greet(step):
        _, where = peer_of(step)
        pl.semaphore_signal(barrier, inc=1, device_id=where, device_id_type=MESH)

    each_peer(greet)

    fetch = [
        pltpu.make_async_copy(spread_hbm.at[gy, gz], spread, tab_sem.at[0]),
        pltpu.make_async_copy(gather_hbm.at[gy, gz], gather, tab_sem.at[1]),
        pltpu.make_async_copy(expand_hbm.at[gx], expand, tab_sem.at[2]),
        pltpu.make_async_copy(shrink_hbm.at[gx], shrink, tab_sem.at[3]),
        pltpu.make_async_copy(scale_hbm, scale, tab_sem.at[4]),
    ]
    for copy in fetch:
        copy.start()

    faces = []
    for bufs, name, index, size, sem in (
        ((s_z, r_z), "gz", gz, n_gz, 0),
        ((s_x, r_x), "gx", gx, n_gx, 2),
    ):
        if size > 1:
            faces.append((*bufs, 0, 1, index > 0, {name: index - 1}, sem))
            faces.append((*bufs, 1, 0, index < size - 1, {name: index + 1}, sem + 1))
    single = n_gy == 2
    if single:
        edge = (ny - 1) * (1 - gy)
        edges = [edge]
        faces.append((s_y, r_y, 0, 0, None, {"gy": 1 - gy}, 4))
    else:
        edges = [0, ny - 1]
        if n_gy > 1:
            faces.append((s_y, r_y, 0, 1, gy > 0, {"gy": gy - 1}, 4))
            faces.append((s_y, r_y, 1, 0, gy < n_gy - 1, {"gy": gy + 1}, 5))

    def copies(turn, landing):
        for src, dst, mine, theirs, exists, where, sem in faces:
            there = sem if single and sem == 4 else (sem // 2) * 2 + theirs
            yield exists, pltpu.make_async_remote_copy(
                src_ref=src.at[turn, mine],
                dst_ref=dst.at[turn, mine if landing else theirs],
                send_sem=send_sem.at[turn, sem],
                recv_sem=recv_sem.at[turn, sem if landing else there],
                device_id=where,
                device_id_type=MESH,
            )

    def guarded(exists, action):
        if exists is None:
            action()
        else:
            pl.when(exists)(action)

    lane = lax.broadcasted_iota(jnp.int32, (nx, ny), 1)
    row = lax.broadcasted_iota(jnp.int32, (nx, ny), 0)
    even = lax.rem(lane + row, 2) == 0
    zero = jnp.zeros((nx, ny), jnp.float32)
    for buf, size, index in ((r_z, n_gz, gz), (r_x, n_gx, gx), (r_y, n_gy, gy)):
        if buf is r_y and single:
            continue
        for side, at in ((0, 0), (1, size - 1)):
            def clear(buf=buf, side=side):
                for turn in range(ROUNDS):
                    buf[turn, side] = jnp.zeros(buf.shape[2:], jnp.float32)

            pl.when(index == at)(clear)

    def slab(z):
        return pl.ds(pl.multiple_of(z * rows, 8) + PAD, nx)

    def packed(packs, value, z):
        result = []
        for pack, at in zip(packs, edges):
            turned = pltpu.roll(value, lax.rem(z - at + ny, ny), 1)
            result.append(jnp.where(lane == z, turned, pack))
        return tuple(result)

    blank = tuple(zero for _ in edges)

    def send(turn, field, packs):
        s_z[turn, 0] = field[pl.ds(rows + PAD, nx), :]
        s_z[turn, 1] = field[pl.ds(pairs * rows + PAD, nx), :]
        for side, at in ((0, PAD), (1, PAD + nx - 1)):
            s_x[turn, side] = field[pl.ds(rows + at, pairs, stride=rows), :]
        for side, pack in enumerate(packs):
            s_y[turn, side] = pack
        for exists, copy in copies(turn, False):
            guarded(exists, copy.start)

    def receive(turn, field):
        for exists, copy in copies(turn, True):
            guarded(exists, copy.wait_recv)
        field[pl.ds(PAD, nx), :] = r_z[turn, 0]
        field[pl.ds((pairs + 1) * rows + PAD, nx), :] = r_z[turn, 1]
        for side, at in ((0, PAD - 1), (1, PAD + nx)):
            field[pl.ds(rows + at, pairs, stride=rows), :] = r_x[turn, side]

    def beside(value, halos, z, strict):
        low, high = pltpu.roll(value, 1, 1), pltpu.roll(value, ny - 1, 1)
        if single:
            halo = pltpu.roll(halos[0], lax.rem(edge - z + ny, ny), 1)
            if strict:
                outer = gy.astype(jnp.float32)
                return (
                    jnp.where(lane == 0, halo * outer, low),
                    jnp.where(lane == ny - 1, halo * (1.0 - outer), high),
                )
            return jnp.where(lane == 0, halo, low), jnp.where(lane == ny - 1, halo, high)
        if n_gy == 1:
            return jnp.where(lane == 0, 0.0, low), jnp.where(lane == ny - 1, 0.0, high)
        first = pltpu.roll(halos[0], lax.rem(ny - z, ny), 1)
        last = pltpu.roll(halos[1], lax.rem(2 * ny - 1 - z, ny), 1)
        return jnp.where(lane == 0, first, low), jnp.where(lane == ny - 1, last, high)

    def around(field, color, halos, z, strict=False):
        same = field[slab(z + 1), :]
        before, after = field[slab(z), :], field[slab(z + 2), :]
        low, high = beside(same, halos, z, strict)
        at = pl.multiple_of((z + 1) * rows, 8) + PAD
        return (
            same,
            jnp.where(even, before, after) if color == 0 else jnp.where(even, after, before),
            field[pl.ds(at - 1, nx), :],
            field[pl.ds(at + 1, nx), :],
            low,
            high,
        )

    def y_halos(turn):
        return [r_y[turn, side] for side in range(len(edges))]

    def loop(count, step, carry, start=0):
        return lax.fori_loop(start, count, step, carry, unroll=UNROLL)

    def conduct(z, packs):
        values = []
        for layer in range(2):
            ids = mat[2 * z + layer]
            value = jnp.full((nx, ny), table[0], jnp.float32)
            for m in range(1, table.shape[0]):
                value = jnp.where(ids == m, table[m], value)
            values.append(value)
        first = jnp.where(even, values[0], values[1])
        second = jnp.where(even, values[1], values[0])
        kr[slab(z + 1), :] = first
        kb[slab(z + 1), :] = second
        return packed(packs[0], first, z), packed(packs[1], second, z)

    inputs[0].wait()
    inputs[1].wait()
    packs = loop(pairs, conduct, (blank, blank))
    pl.semaphore_wait(barrier, count - 1)
    send(0, kr, packs[0])
    send(1, kb, packs[1])
    inputs[2].wait()
    receive(0, kr)
    receive(1, kb)

    def quiet(field):
        field[pl.ds(PAD, nx), :] = zero
        field[pl.ds((pairs + 1) * rows + PAD, nx), :] = zero
        for at in (PAD - 1, PAD + nx):
            field[pl.ds(rows + at, pairs, stride=rows), :] = jnp.zeros((pairs, ny), jnp.float32)

    def weigh(color, own, field, turn, first):
        halos = y_halos(turn)

        def step(z, carry):
            packs, edge_packs = carry
            center = own[slab(z + 1), :]
            others = around(field, color, halos, z, True)
            diag = None
            inner = []
            for other in others:
                inside = other > 0.0
                weight = 2.0 * center * other / (center + other)
                full = jnp.where(inside, weight, center)
                inner.append(jnp.where(inside, weight, 0.0))
                diag = full if diag is None else diag + full
            inverse = 1.0 / diag
            for face in range(6):
                inner[face] = inner[face] * inverse
                wd[color, face, z] = inner[face]
            wxf[color, 0, pl.ds(z, 1), :] = inner[2][:1]
            wxf[color, 1, pl.ds(z, 1), :] = inner[3][nx - 1 :]
            edge_packs = packed(edge_packs, jnp.where(lane == 0, inner[4], inner[5]), z)
            lower, upper = heat[2 * z], heat[2 * z + 1]
            source = jnp.where(even, lower, upper) if color == 0 else jnp.where(even, upper, lower)
            ratio = source * inverse
            hd[color, z] = ratio
            dg[color, z] = diag
            if not first:
                return packs, edge_packs
            red[slab(z + 1), :] = ratio
            return packed(packs, ratio, z), edge_packs

        packs, edge_packs = loop(pairs, step, (blank, blank))
        for side, pack in enumerate(edge_packs):
            wyf[color, side] = pack
        return packs

    quiet(red)
    packs = weigh(0, kr, kb, 1, True)
    send(2, red, packs)
    weigh(1, kb, kr, 0, False)

    def total(color, field, halos, z):
        others = around(field, color, halos, z)
        result = hd[color, z]
        for face in range(6):
            result = result + wd[color, face, z] * others[face]
        return result

    def early(color, halos=blank):
        field = (black, red)[color]

        def step(z, carry):
            ahead[slab(z + 1), :] = total(color, field, halos, z)
            return carry

        loop(pairs, step, 0)

    def late(turn, color, store, carry):
        for exists, copy in copies(turn, True):
            guarded(exists, copy.wait_recv)
        for side, z in ((0, 0), (1, pairs - 1)):
            term = wd[color, 1, z] * r_z[turn, side]
            mine = even if side == color else jnp.logical_not(even)
            ahead[slab(z + 1), :] = ahead[slab(z + 1), :] + jnp.where(mine, term, 0.0)
        for side, at in ((0, PAD), (1, PAD + nx - 1)):
            where = pl.ds(rows + at, pairs, stride=rows)
            ahead[where, :] = ahead[where, :] + wxf[color, side] * r_x[turn, side]
        terms = [wyf[color, side] * r_y[turn, side] for side in range(len(edges))]

        def step(z, carry):
            value = ahead[slab(z + 1), :]
            for term, at in zip(terms, edges):
                term = pltpu.roll(term, lax.rem(at - z + ny, ny), 1)
                value = jnp.where(lane == at, value + term, value)
            return store(z, value, carry)

        return lax.fori_loop(0, pairs, step, carry, unroll=2 * UNROLL)

    def finished(turn, color):
        own = (red, black)[color]

        def store(z, value, packs):
            own[slab(z + 1), :] = value
            return packed(packs, value, z)

        return late(turn, color, store, blank)

    quiet(black)
    for turn, color in ((3, 1), (4, 0), (5, 1)):
        early(color)
        packs = finished(turn - 1, color)
        send(turn, (red, black)[color], packs)

    vsum[...] = jnp.zeros(vsum.shape, jnp.float32)
    tile = jnp.zeros((8, ny), jnp.float32)
    tile_row = lax.broadcasted_iota(jnp.int32, (8, ny), 0)

    def outward(z):
        return dg[1, z] * black[slab(z + 1), :]

    for layer in range(lz):
        def gap(z, sums):
            inner, low, high, ends = sums
            flow = outward(z)
            inner = inner + dg[0, z] * (total(0, black, blank, z) - red[slab(z + 1), :])
            low = low + (wd[1, 2, z] * flow)[:8]
            high = high + (wd[1, 3, z] * flow)[nx - 8 :]
            weight = jnp.where(lane == 0, wd[1, 4, z], jnp.where(lane == ny - 1, wd[1, 5, z], 0.0))
            return inner, low, high, ends + weight * flow

        inner, low, high, ends = loop(
            (layer + 1) * BLOCK // 2, gap, (zero, tile, tile, zero), layer * BLOCK // 2
        )
        here = slice((layer + 1) * ny, (layer + 2) * ny)
        vsum[PAD : PAD + nx, here] = inner
        vsum[PAD - 8 : PAD, here] = jnp.where(tile_row == 7, pltpu.roll(low, 7, 0), 0.0)
        vsum[PAD + nx : PAD + nx + 8, here] = jnp.where(tile_row == 0, pltpu.roll(high, 1, 0), 0.0)
        vsum[PAD : PAD + nx, (lz + 2 + layer) * ny : (lz + 3 + layer) * ny] = ends
    vsum[PAD : PAD + nx, :ny] = jnp.where(even, 0.0, wd[1, 1, 0] * outward(0))
    vsum[PAD : PAD + nx, (lz + 1) * ny : (lz + 2) * ny] = jnp.where(
        even, wd[1, 1, pairs - 1] * outward(pairs - 1), 0.0
    )
    for copy in fetch:
        copy.wait()
    part = jnp.dot(shrink[...], vsum[...], precision=HIGH, preferred_element_type=jnp.float32)
    part = jnp.dot(part, gather[...], precision=HIGH, preferred_element_type=jnp.float32)
    got[me] = part

    def gathering(step, start):
        other, where = peer_of(step)
        copy = pltpu.make_async_remote_copy(
            src_ref=got.at[me],
            dst_ref=got.at[me if start else other],
            send_sem=gsend.at[step],
            recv_sem=grecv.at[me if start else other],
            device_id=where,
            device_id_type=MESH,
        )
        return copy

    each_peer(lambda step: gathering(step, True).start())
    each_peer(lambda step: gathering(step, False).wait_recv())
    if count <= 32:
        hat = got[0]
        for i in range(1, count):
            hat = hat + got[i]
    else:
        hat = lax.fori_loop(1, count, lambda i, acc: acc + got[i], got[0])
    kbar = table[0]
    for m in range(1, table.shape[0]):
        kbar = kbar + table[m]
    kbar = kbar / table.shape[0]
    hat = hat * scale[...] / kbar
    hat = jnp.dot(hat, spread[...], precision=HIGH, preferred_element_type=jnp.float32)
    corr[...] = jnp.dot(expand[...], hat, precision=HIGH, preferred_element_type=jnp.float32)

    def correct(z, carry):
        layer = (z + BLOCK // 2 - 1) // (BLOCK // 2)
        at = pl.ds(pl.multiple_of(z * rows, 8), rows)
        black[at, :] = black[at, :] + corr[:, pl.ds(pl.multiple_of(layer * ny, ny), ny)]
        return carry

    lax.fori_loop(0, pairs + 2, correct, 0, unroll=2)
    sides = [corr[PAD : PAD + nx, (lz + 2 + s) * ny : (lz + 3 + s) * ny] for s in range(2)]
    if single:
        upper = gy.astype(jnp.float32)
        sides = [sides[0] * upper + sides[1] * (1.0 - upper)]
    early(0, sides)
    quiet(black)
    packs = finished(5, 0)
    send(6, red, packs)
    for turn, color in ((7, 1), (8, 0)):
        early(color)
        packs = finished(turn - 1, color)
        send(turn, (red, black)[color], packs)
    early(1)

    def finish(z, last, carry):
        own = red[slab(z + 1), :]
        out[2 * z] = jnp.where(even, own, last)
        out[2 * z + 1] = jnp.where(even, last, own)
        return carry

    late(8, 1, finish, 0)

    for turn in range(ROUNDS):
        for exists, copy in copies(turn, False):
            guarded(exists, copy.wait_send)

    each_peer(lambda step: gathering(step, True).wait_send())


def per_device(sizes, heat, material, table):
    shape = heat.shape
    nz, nx, ny = shape
    n_gx, n_gy, n_gz = sizes
    consts = tables(shape, *sizes)
    spread, gather, expand, shrink, scale = consts
    count = n_gx * n_gy * n_gz
    rows = nx + 2 * PAD
    sides = 1 if n_gy == 2 else 2
    f32 = jnp.float32
    vmem = pl.BlockSpec(memory_space=pltpu.VMEM)
    hbm = pl.BlockSpec(memory_space=pltpu.HBM)
    faces = [
        pltpu.VMEM((ROUNDS, 2, nx, ny), f32),
        pltpu.VMEM((ROUNDS, 2, nx, ny), f32),
        pltpu.VMEM((ROUNDS, 2, nz // 2, ny), f32),
        pltpu.VMEM((ROUNDS, 2, nz // 2, ny), f32),
        pltpu.VMEM((ROUNDS, sides, nx, ny), f32),
        pltpu.VMEM((ROUNDS, sides, nx, ny), f32),
    ]
    return pl.pallas_call(
        functools.partial(kernel, sizes, shape),
        out_shape=jax.ShapeDtypeStruct(shape, f32),
        in_specs=[hbm] * 8,
        out_specs=vmem,
        scratch_shapes=[
            pltpu.VMEM(shape, f32),
            pltpu.VMEM(shape, jnp.int32),
            pltpu.SMEM(table.shape, f32),
            *[pltpu.VMEM(((nz // 2 + 2) * rows, ny), f32)] * 5,
            pltpu.VMEM((2, 6, nz // 2, nx, ny), f32),
            pltpu.VMEM((2, 2, nz // 2, ny), f32),
            pltpu.VMEM((2, sides, nx, ny), f32),
            pltpu.VMEM((2, nz // 2, nx, ny), f32),
            pltpu.VMEM((2, nz // 2, nx, ny), f32),
            pltpu.VMEM((rows, gather.shape[2]), f32),
            pltpu.VMEM((rows, spread.shape[3]), f32),
            pltpu.VMEM(spread.shape[2:], f32),
            pltpu.VMEM(gather.shape[2:], f32),
            pltpu.VMEM(expand.shape[1:], f32),
            pltpu.VMEM(shrink.shape[1:], f32),
            pltpu.VMEM(scale.shape, f32),
            *faces,
            pltpu.VMEM((count, *scale.shape), f32),
            pltpu.SemaphoreType.DMA((8,)),
            pltpu.SemaphoreType.DMA((ROUNDS, 6)),
            pltpu.SemaphoreType.DMA((ROUNDS, 6)),
            pltpu.SemaphoreType.DMA((count,)),
            pltpu.SemaphoreType.DMA((count,)),
        ],
        compiler_params=pltpu.CompilerParams(
            collective_id=0, has_side_effects=True, vmem_limit_bytes=64 * 1024 * 1024
        ),
    )(heat, material, table, *(jnp.asarray(c) for c in consts))


def solution(mesh):
    sizes = (mesh.shape["gx"], mesh.shape["gy"], mesh.shape["gz"])
    spec = P("gz", ("groups", "gx"), "gy")
    return jax.shard_map(
        functools.partial(per_device, sizes),
        mesh=mesh,
        in_specs=(spec, spec, P()),
        out_specs=spec,
        check_vma=False,
    )
```
